128 devices in a mesh: row: 16 (over y, z), col: 8 (over x, core).
Axes of the slice: x: 4, y: 4, z: 4, core: 2. Of those that a mesh axis runs over, the one named last changes fastest.
Arguments:
- block_cols: int32 [64, 16], replicated, may hold values from -1 to 63, as said below
- step_dir: bfloat16 [64, 16, 128, 128], P('row', 'col')
- intersection: bfloat16 [64, 16, 128, 128], P('row', 'col')
- density: bfloat16 [64, 16, 128, 128], P('row', 'col')
- kohn_sham: bfloat16 [64, 16, 128, 128], P('row', 'col')
Outputs:
- commutator: bfloat16 [64, 16, 128, 128], P('row', 'col')
- trace_value: float32 [], replicated
The draws below stay inside these ranges and needn't reach their ends.
Inputs may be any that keep to these rules, and one draw needn't show every extreme that they name: block_cols[i, s] is -1 or a block column of group s // 2, that is from (s // 2) * 8 to (s // 2 + 1) * 8 - 1; the live entries of one block row within one group are distinct; the pattern is symmetric (j is live in row i exactly when i is live in row j) and holds every diagonal block.
All inputs are finite; a program needn't handle non-finite values.
Results may differ from the reference program's by a relative error of at most 0.0057.
Values may be sent and summed in bfloat16 or wider, within the bound.
A program may use at most 64 MiB of HBM per device.

```python
import jax
import jax.numpy as jnp
from jax import lax

BLK = 128
KS = 2
NB = 64
GROUP = 8
KT = 16


def build_pattern(key):
    tile_count = NB // GROUP
    perm_keys = jax.random.split(jax.random.fold_in(key, 1), tile_count * tile_count)
    permuted = jax.vmap(lambda sub_key: jax.random.permutation(sub_key, GROUP))(perm_keys).reshape(tile_count, tile_count, GROUP)
    keep_flags = jax.random.randint(jax.random.fold_in(key, 2), (NB, tile_count, KS), 0, 2)
    row_ids = jnp.arange(NB)
    tile_row = row_ids // GROUP
    local_row = row_ids % GROUP
    keep_flags = jnp.where(local_row[:, None, None] == 0, 1, keep_flags)
    shift_ids = jnp.arange(KS)
    shift_pos = (local_row[:, None] + shift_ids[None, :]) % GROUP
    targets = permuted[tile_row[:, None, None], jnp.arange(tile_count)[None, :, None], shift_pos[:, None, :]]
    hit_mask = (targets[..., None] == jnp.arange(GROUP)[None, None, None, :]) & (keep_flags[..., None] == 1)
    full_mask = jnp.any(hit_mask, axis=2).reshape(NB, NB)
    half_count = (KS - 1) // 2
    half_mask = jnp.any(hit_mask & (shift_ids[None, None, :, None] < half_count), axis=2).reshape(NB, NB)
    tile_left = tile_row[:, None]
    tile_right = tile_row[None, :]
    on_diagonal = row_ids[:, None] == row_ids[None, :]
    inner_mask = half_mask | half_mask.T | on_diagonal
    return jnp.where(tile_left < tile_right, full_mask, jnp.where(tile_left > tile_right, full_mask.T, inner_mask))


def draw_block_cols(key, part):
    sym_mask = build_pattern(jax.random.fold_in(key, 11))
    tile_count = NB // GROUP
    grouped = sym_mask.reshape(NB, tile_count, GROUP)
    local_ids = jnp.arange(GROUP, dtype=jnp.int32)
    scores = jnp.where(grouped, local_ids, GROUP + local_ids)
    slot_order = jnp.argsort(scores, axis=-1, stable=True)[..., :KS]
    is_live = jnp.take_along_axis(grouped, slot_order, axis=-1)
    column = jnp.arange(tile_count, dtype=jnp.int32)[None, :, None] * GROUP + slot_order
    return jnp.where(is_live, column, -1).reshape(NB, tile_count * KS).astype(jnp.int32)


def diagonal_blocks(key, part):
    pattern = draw_block_cols(key, part)
    on_diagonal = (pattern == jnp.arange(NB, dtype=jnp.int32)[:, None]).astype(jnp.float32)
    return on_diagonal[:, :, None, None] * jnp.eye(BLK, dtype=jnp.float32)[None, None, :, :]


def fock_unit(key):
    values = jnp.clip(jax.random.normal(jax.random.fold_in(key, 31), (NB, KT, BLK, BLK), jnp.float32), -3.0, 3.0)
    return values


def draw_kohn_sham(key, part):
    spread = (BLK * KT // 2) ** (-0.5)
    return (fock_unit(key) * spread).astype(jnp.bfloat16)


def draw_intersection(key, part):
    spread = (BLK * KT // 2) ** (-0.5)
    values = jnp.clip(jax.random.normal(jax.random.fold_in(key, 21), (NB, KT, BLK, BLK), jnp.float32), -4.0, 4.0)
    return (values * spread + diagonal_blocks(key, part)).astype(jnp.bfloat16)


def draw_density(key, part):
    spread = (BLK * KT // 2) ** (-0.5)
    values = jnp.clip(jax.random.normal(jax.random.fold_in(key, 22), (NB, KT, BLK, BLK), jnp.float32), -4.0, 4.0)
    return (values * spread + 0.5 * diagonal_blocks(key, part)).astype(jnp.bfloat16)


def draw_step_dir(key, part):
    row_ids = jnp.arange(NB).astype(jnp.float32)
    noise_vals = jnp.clip(jax.random.normal(jax.random.fold_in(key, 41), (NB, KT, BLK, BLK), jnp.float32), -3.0, 3.0)
    row_ramp = 1.0 + 2.0 * row_ids / (NB - 1)
    mixed = 0.6 * fock_unit(key) + 0.8 * noise_vals
    return (mixed * row_ramp[:, None, None, None]).astype(jnp.bfloat16)


def setup_inputs(seed: int = 0) -> dict:
    splits = jax.random.split(jax.random.key(seed), 6)
    return {
        "block_cols": draw_block_cols(jax.random.fold_in(splits[5], 71), 0),
        "step_dir": draw_step_dir(jax.random.fold_in(splits[5], 71), 0),
        "intersection": draw_intersection(jax.random.fold_in(splits[5], 71), 0),
        "density": draw_density(jax.random.fold_in(splits[5], 71), 0),
        "kohn_sham": draw_kohn_sham(jax.random.fold_in(splits[5], 71), 0),
    }


def product(left_blocks, right_blocks, block_cols):
    def one_row(row_args):
        row_cols, row_left = row_args
        target_rows = jnp.clip(row_cols, 0, NB - 1).astype(jnp.int32)
        right_rows = right_blocks[target_rows].astype(jnp.float32)
        right_cols = block_cols[target_rows]
        matched = (right_cols[:, None, :] == row_cols[None, :, None]) & (row_cols[None, :, None] >= 0) & (row_cols[:, None, None] >= 0)
        picked = jnp.einsum('tab,tbqr->taqr', matched.astype(jnp.float32), right_rows, precision=lax.Precision.HIGHEST)
        return jnp.einsum('apr,taqr->tpq', row_left.astype(jnp.float32), picked, precision=lax.Precision.HIGHEST)

    return lax.map(one_row, (block_cols, left_blocks))


def reference(block_cols, step_dir, intersection, density, kohn_sham):
    scaled_step = product(step_dir, intersection, block_cols).astype(jnp.bfloat16)
    summed = product(scaled_step, density, block_cols) + product(density, scaled_step, block_cols)
    change = (-summed).astype(jnp.bfloat16)
    difference = product(kohn_sham, change, block_cols) - product(change, kohn_sham, block_cols)
    commutator = difference.astype(jnp.bfloat16)
    trace_value = jnp.sum(change.astype(jnp.float32) * kohn_sham.astype(jnp.float32)) / (NB * BLK * BLK)
    return commutator, trace_value
```

```python
import jax
import jax.numpy as jnp
from jax import lax
from jax.experimental import pallas as pl
from jax.experimental.pallas import tpu as pltpu
from jax.sharding import PartitionSpec as P

MESH = pl.DeviceIdType.MESH
BF = jnp.bfloat16
F32 = jnp.float32
ZERO = 128
TZERO = 16


def kernel(
    cols, step, inter, dens, fock, out, trace,
    r_i, r_d, r_k, l_p, l_s, l_c, parts, landed, own, x_send, x_recv0, x_recv1, t_src, t_buf, pick, tpick,
    p1_send, p1_recv_a, p1_recv_b, p1_local, p2_send, p2_recv_a, p2_recv_b,
    l_send, l_recv, l_local, rs_send, rs_recv, x_ssem, x_rsem, x_local, t_send, t_recv,
):
    row = lax.axis_index("row")
    col = lax.axis_index("col")
    x, k = col // 2, col % 2
    y, z = row // 4, row % 4
    h = z // 2
    zz = z % 2

    x_recv = (x_recv0, x_recv1)

    def dev(x_, k_, y_, z_):
        return (y_ * 4 + z_, x_ * 2 + k_)

    def remote(src, dst, ssem, rsem, target):
        return pltpu.make_async_remote_copy(src, dst, ssem, rsem, device_id=target, device_id_type=MESH)

    barrier = pltpu.get_barrier_semaphore()
    for d in range(1, 8):
        pl.semaphore_signal(barrier, 1, device_id=(row, (col + d) % 8), device_id_type=MESH)
    for d in range(1, 4):
        for kk in range(2):
            pl.semaphore_signal(barrier, 1, device_id=dev(x, kk, (y + d) % 4, z), device_id_type=MESH)
            pl.semaphore_signal(barrier, 1, device_id=dev(x, kk, y, (z + d) % 4), device_id_type=MESH)
    for q in range(2):
        is_self = (x == y) & (k == h) & (zz == q)

        @pl.when(jnp.logical_not(is_self))
        def _():
            pl.semaphore_signal(barrier, 1, device_id=dev(y, h, x, 2 * k + q), device_id_type=MESH)

    r_i[ZERO] = jnp.zeros((128, 128), BF)
    r_d[ZERO] = jnp.zeros((128, 128), BF)
    r_k[ZERO] = jnp.zeros((128, 128), BF)
    x_recv0[TZERO] = jnp.zeros((128, 128), BF)
    x_recv1[TZERO] = jnp.zeros((128, 128), BF)
    pl.semaphore_wait(barrier, 21 - jnp.where((x == y) & (k == h), 1, 0))

    gathers = ((inter, r_i), (dens, r_d), (fock, r_k))

    def p1_copy(m, d):
        tile, buf = gathers[m]
        slot_a = (y * 2 + zz) * 8
        slot_b = (8 + zz * 4 + y) * 8
        kind, off = d
        if kind == "a":
            return remote(tile, buf.at[pl.ds(slot_a, 8)], p1_send.at[m, off], p1_recv_a.at[m, zz], dev(x, h, y, (z + off) % 4))
        return remote(tile, buf.at[pl.ds(slot_b, 8)], p1_send.at[m, off], p1_recv_b.at[m, y], dev(x, h, (y + off) % 4, z))

    def p1_local_copy(m):
        tile, buf = gathers[m]
        slot = jnp.where(k == 0, y * 2 + zz, 8 + zz * 4 + y) * 8
        return pltpu.make_async_copy(tile, buf.at[pl.ds(slot, 8)], p1_local.at[m])

    def p1_start(m):
        for off in (1, 3, 2, 0):
            go = (k != h) if off == 0 else True

            @pl.when((k == 0) & go)
            def _():
                p1_copy(m, ("a", off)).start()

            @pl.when((k == 1) & go)
            def _():
                p1_copy(m, ("b", off)).start()

        @pl.when(k == h)
        def _():
            p1_local_copy(m).start()

    def p1_wait_send(m):
        for off in (1, 3, 2, 0):
            go = (k != h) if off == 0 else True

            @pl.when((k == 0) & go)
            def _():
                p1_copy(m, ("a", off)).wait_send()

            @pl.when((k == 1) & go)
            def _():
                p1_copy(m, ("b", off)).wait_send()

    def recv_wait(buf, start, n, sem):
        view = buf.at[pl.ds(start, n)]
        remote(view, view, sem, sem, dev(x, 1 - k, y, z)).wait_recv()

    def p1_wait(m):
        tile, buf = gathers[m]

        @pl.when(k == h)
        def _():
            p1_local_copy(m).wait()

        for q in range(2):
            mine = (k == 0) & (h == 0) & (zz == q)

            @pl.when(jnp.logical_not(mine))
            def _():
                recv_wait(buf, (y * 2 + q) * 8, 8, p1_recv_a.at[m, q])

        for yy in range(4):
            mine = (k == 1) & (y == yy)

            @pl.when((k == h) & jnp.logical_not(mine))
            def _():
                recv_wait(buf, (8 + zz * 4 + yy) * 8, 8, p1_recv_b.at[m, yy])

    def p2_a(m, off):
        buf = gathers[m][1]
        view = buf.at[pl.ds(y * 16, 16)]
        return remote(view, view, p2_send.at[m, 0, off], p2_recv_a.at[m, y], dev(x, k, (y + off) % 4, z))

    def p2_b(m, off):
        buf = gathers[m][1]
        view = buf.at[pl.ds(64 + zz * 32, 32)]
        return remote(view, view, p2_send.at[m, 1, off], p2_recv_b.at[m, zz], dev(x, k, y, (z + off) % 4))

    def p2_start(m):
        for off in (2, 1, 3):
            p2_a(m, off).start()

            @pl.when(k == h)
            def _():
                p2_b(m, off).start()

    def p2_wait(m):
        buf = gathers[m][1]
        for yy in range(4):
            @pl.when(y != yy)
            def _():
                recv_wait(buf, yy * 16, 16, p2_recv_a.at[m, yy])
        for q in range(2):
            @pl.when(jnp.logical_not((k == h) & (zz == q)))
            def _():
                recv_wait(buf, 64 + q * 32, 32, p2_recv_b.at[m, q])

    def p2_wait_send(m):
        for off in (2, 1, 3):
            p2_a(m, off).wait_send()

            @pl.when(k == h)
            def _():
                p2_b(m, off).wait_send()

    def l_swap(n, src, buf):
        return remote(src, buf.at[k], l_send.at[n], l_recv.at[n], dev(x, 1 - k, y, z))

    l_swap(0, step, l_p).start()
    pltpu.make_async_copy(step, l_p.at[k], l_local.at[0]).start()
    p1_start(0)
    p1_start(1)
    p1_start(2)

    base = row * 4

    def make_pick(n, carry):
        i, t, s = n // 8, (n // 2) % 4, n % 2
        j = cols[base + i, (2 * t + k) * 2 + s]
        jj = jnp.maximum(j, 0)
        w, q = jj & 3, (jj >> 2) & 1
        for a in range(4):
            c = a // 2
            kk = cols[base + i, 4 * x + a]
            tile = t * 2 + q if c == 0 else 8 + q * 4 + t
            block = tile * 8 + w * 2
            live = (j >= 0) & (kk >= 0)
            first = cols[jj, 4 * x + 2 * c]
            second = cols[jj, 4 * x + 2 * c + 1]
            got = jnp.where(first == kk, block, jnp.where(second == kk, block + 1, ZERO))
            pick[n * 4 + a] = jnp.where(live, got, ZERO)
        return carry

    def make_tpick(n, carry):
        i, s = n // 2, n % 2
        j = cols[base + i, col * 2 + s]
        jj = jnp.maximum(j, 0)
        w, q = jj & 3, (jj >> 2) & 1
        block = q * 8 + w * 2
        g = (2 * y + h) * 2
        first = cols[jj, g]
        second = cols[jj, g + 1]
        got = jnp.where(first == base + i, block, jnp.where(second == base + i, block + 1, TZERO))
        tpick[n] = jnp.where(j >= 0, got, TZERO)
        return carry

    lax.fori_loop(0, 32, make_pick, 0)
    lax.fori_loop(0, 8, make_tpick, 0)

    for m in range(3):
        p1_wait(m)
        p2_start(m)

    def rs_copy(n, off):
        return remote(
            parts.at[n, (x + off) % 4], landed.at[n, off], rs_send.at[n, off], rs_recv.at[n, off],
            dev((x + off) % 4, k, y, z),
        )

    def stage(n, left, right):
        for off in (2, 1, 3, 0):
            t = (x + off) % 4

            def one_row(i, carry):
                lhs = jnp.concatenate([left[a // 2, i * 2 + a % 2] for a in range(4)], axis=1)
                rhs = jnp.concatenate(
                    [
                        jnp.concatenate([right[pick[((i * 4 + t) * 2 + s) * 4 + a]] for a in range(4)], axis=1)
                        for s in range(2)
                    ],
                    axis=0,
                )
                got = lax.dot_general(lhs, rhs, (((1,), (1,)), ((), ())), preferred_element_type=F32)
                for s in range(2):
                    block = got[:, s * 128 : (s + 1) * 128]
                    if off == 0:
                        own[n, i * 2 + s] = block
                    else:
                        parts[n, t, i * 2 + s] = block.astype(BF)
                return carry

            lax.fori_loop(0, 4, one_row, 0)
            if off != 0:
                rs_copy(n, off).start()

    def rs_wait(n):
        for off in (1, 3, 2):
            rs_copy(n, off).wait()

    def total(n, b):
        acc = own[n, b]
        for off in (1, 3, 2):
            acc = acc + landed[n, off, b].astype(F32)
        return acc

    def x_copy(n, q):
        return remote(
            x_send.at[n], x_recv[n].at[pl.ds(zz * 8, 8)], x_ssem.at[n, q], x_rsem.at[n, zz],
            dev(y, h, x, 2 * k + q),
        )

    def x_local_copy(n):
        return pltpu.make_async_copy(x_send.at[n], x_recv[n].at[pl.ds(zz * 8, 8)], x_local.at[n])

    def x_self(q):
        return (x == y) & (k == h) & (zz == q)

    def x_start(n):
        for q in range(2):
            @pl.when(jnp.logical_not(x_self(q)))
            def _():
                x_copy(n, q).start()

            @pl.when(x_self(q))
            def _():
                x_local_copy(n).start()

    def x_wait(n):
        for q in range(2):
            @pl.when(jnp.logical_not(x_self(q)))
            def _():
                x_copy(n, q).wait_send()
                recv_wait(x_recv[n], q * 8, 8, x_rsem.at[n, q])

            @pl.when(x_self(q))
            def _():
                x_local_copy(n).wait()

    def flipped(n, b):
        return x_recv[n][tpick[b]].astype(F32).T

    pltpu.make_async_copy(step, l_p.at[k], l_local.at[0]).wait()
    l_swap(0, step, l_p).wait()
    p2_wait(0)
    stage(0, l_p, r_i)
    rs_wait(0)

    def s_block(b, carry):
        l_s[k, b] = total(0, b).astype(BF)
        return carry

    lax.fori_loop(0, 8, s_block, 0)
    l_swap(1, l_s.at[k], l_s).start()
    p2_wait(1)
    l_swap(1, l_s.at[k], l_s).wait()

    stage(1, l_s, r_d)
    rs_wait(1)

    def x_block(b, carry):
        v = total(1, b)
        own[1, b] = v
        x_send[0, b] = v.astype(BF)
        return carry

    lax.fori_loop(0, 8, x_block, 0)
    x_start(0)
    x_wait(0)

    def c_block(b, acc):
        c = (-(own[1, b] + flipped(0, b))).astype(BF)
        l_c[k, b] = c
        prod = c.astype(F32) * fock[b].astype(F32)
        return acc + prod.reshape(16, 8, 128).sum(axis=0)

    tsum = lax.fori_loop(0, 8, c_block, jnp.zeros((8, 128), F32))
    l_swap(2, l_c.at[k], l_c).start()

    def t_copy(level, off):
        if level == 0:
            target, slot = (row, (col + off) % 8), col
        elif level == 1:
            target, slot = dev(x, k, (y + off) % 4, z), y
        else:
            target, slot = dev(x, k, y, (z + off) % 4), z
        return remote(t_src.at[level], t_buf.at[level, slot], t_send.at[level, off], t_recv.at[level, slot], target)

    sizes = (8, 4, 4)
    mine = (col, y, z)

    def t_start(level, value):
        t_src[level] = value
        for off in range(1, sizes[level]):
            t_copy(level, off).start()

    def t_finish(level, value):
        acc = jnp.zeros((8, 128), F32)
        for q in range(sizes[level]):
            @pl.when(mine[level] != q)
            def _():
                remote(
                    t_src.at[level], t_buf.at[level, q], t_recv.at[level, q], t_recv.at[level, q], dev(x, 1 - k, y, z)
                ).wait_recv()

        for off in range(1, sizes[level]):
            t_copy(level, off).wait_send()
        for q in range(sizes[level]):
            acc = acc + jnp.where(mine[level] == q, value, t_buf[level, q])
        return acc

    t_start(0, tsum)
    p2_wait(2)
    l_swap(2, l_c.at[k], l_c).wait()

    stage(2, l_c, r_k)
    tsum = t_finish(0, tsum)
    t_start(1, tsum)
    rs_wait(2)

    def w_block(b, carry):
        v = total(2, b)
        own[2, b] = v
        x_send[1, b] = v.astype(BF)
        return carry

    lax.fori_loop(0, 8, w_block, 0)
    x_start(1)
    tsum = t_finish(1, tsum)
    t_start(2, tsum)
    for m in range(3):
        p1_wait_send(m)
        p2_wait_send(m)
    tsum = t_finish(2, tsum)
    trace[0, 0] = jnp.sum(tsum) * (1.0 / 1048576.0)
    x_wait(1)

    def o_block(b, carry):
        out[b] = (flipped(1, b) - own[2, b]).astype(BF)
        return carry

    lax.fori_loop(0, 8, o_block, 0)


def per_device(block_cols, step_dir, intersection, density, kohn_sham):
    flat = lambda a: a.reshape(8, 128, 128)
    vmem = pl.BlockSpec(memory_space=pltpu.VMEM)
    smem = pl.BlockSpec(memory_space=pltpu.SMEM)
    dma = pltpu.SemaphoreType.DMA
    blk = (128, 128)
    out, trace = pl.pallas_call(
        kernel,
        out_shape=(jax.ShapeDtypeStruct((8, 128, 128), BF), jax.ShapeDtypeStruct((1, 1), F32)),
        in_specs=[smem, vmem, vmem, vmem, vmem],
        out_specs=(vmem, smem),
        scratch_shapes=[
            pltpu.VMEM((129,) + blk, BF), pltpu.VMEM((129,) + blk, BF), pltpu.VMEM((129,) + blk, BF),
            pltpu.VMEM((2, 8) + blk, BF), pltpu.VMEM((2, 8) + blk, BF), pltpu.VMEM((2, 8) + blk, BF),
            pltpu.VMEM((3, 4, 8) + blk, BF), pltpu.VMEM((3, 4, 8) + blk, BF), pltpu.VMEM((3, 8) + blk, F32),
            pltpu.VMEM((2, 8) + blk, BF), pltpu.VMEM((17,) + blk, BF), pltpu.VMEM((17,) + blk, BF),
            pltpu.VMEM((3, 8, 128), F32), pltpu.VMEM((3, 8, 8, 128), F32),
            pltpu.SMEM((128,), jnp.int32), pltpu.SMEM((8,), jnp.int32),
            dma((3, 4)), dma((3, 2)), dma((3, 4)), dma((3,)), dma((3, 2, 4)), dma((3, 4)), dma((3, 2)),
            dma((3,)), dma((3,)), dma((1,)), dma((3, 4)), dma((3, 4)), dma((2, 2)), dma((2, 2)), dma((2,)),
            dma((3, 8)), dma((3, 8)),
        ],
        compiler_params=pltpu.CompilerParams(
            collective_id=0, has_side_effects=True, vmem_limit_bytes=48 * 2**20
        ),
        name="hessian",
    )(block_cols, flat(step_dir), flat(intersection), flat(density), flat(kohn_sham))
    return out.reshape(4, 2, 128, 128), trace.reshape(())


def solution(mesh):
    spec = P("row", "col", None, None)
    return jax.shard_map(
        per_device, mesh=mesh, in_specs=(P(), spec, spec, spec, spec), out_specs=(spec, P()), check_vma=False
    )
```

```python
import jax
import jax.numpy as jnp
from jax import lax
from jax.experimental import pallas as pl
from jax.experimental.pallas import tpu as pltpu
from jax.sharding import PartitionSpec as P

MESH = pl.DeviceIdType.MESH
BF = jnp.bfloat16
F32 = jnp.float32
ZERO = 128
TZERO = 16


def kernel(
    cols, step, inter, dens, fock, out, trace,
    r_i, r_d, r_k, l_p, l_s, l_c, parts, landed, own, x_send, x_recv0, x_recv1, t_src, t_buf, pick, tpick,
    p1_send, p1_recv_a, p1_recv_b, p1_local, p2_send, p2_recv_a, p2_recv_b,
    l_send, l_recv, l_local, rs_send, rs_recv, x_ssem, x_rsem, x_local, relay, rl_ssem, rl_rsem, rl_fsem, t_send, t_recv,
):
    row = lax.axis_index("row")
    col = lax.axis_index("col")
    x, k = col // 2, col % 2
    y, z = row // 4, row % 4
    h = z // 2
    zz = z % 2

    x_recv = (x_recv0, x_recv1)

    def dev(x_, k_, y_, z_):
        return (y_ * 4 + z_, x_ * 2 + k_)

    def remote(src, dst, ssem, rsem, target):
        return pltpu.make_async_remote_copy(src, dst, ssem, rsem, device_id=target, device_id_type=MESH)

    barrier = pltpu.get_barrier_semaphore()
    for d in range(1, 8):
        pl.semaphore_signal(barrier, 1, device_id=(row, (col + d) % 8), device_id_type=MESH)
    for d in range(1, 4):
        for kk in range(2):
            pl.semaphore_signal(barrier, 1, device_id=dev(x, kk, (y + d) % 4, z), device_id_type=MESH)
            pl.semaphore_signal(barrier, 1, device_id=dev(x, kk, y, (z + d) % 4), device_id_type=MESH)
    for q in range(2):
        is_self = (x == y) & (k == h) & (zz == q)

        @pl.when(jnp.logical_not(is_self))
        def _():
            pl.semaphore_signal(barrier, 1, device_id=dev(y, h, x, 2 * k + q), device_id_type=MESH)

    for q in range(2):
        @pl.when((h == 1) & (x != y))
        def _():
            pl.semaphore_signal(barrier, 1, device_id=dev(y, 1, y, 2 * k + q), device_id_type=MESH)

    r_i[ZERO] = jnp.zeros((128, 128), BF)
    r_d[ZERO] = jnp.zeros((128, 128), BF)
    r_k[ZERO] = jnp.zeros((128, 128), BF)
    x_recv0[TZERO] = jnp.zeros((128, 128), BF)
    x_recv1[TZERO] = jnp.zeros((128, 128), BF)
    pl.semaphore_wait(barrier, 21 - jnp.where((x == y) & (k == h), 1, 0) + jnp.where((x == y) & (k == 1), 6, 0))

    gathers = ((inter, r_i), (dens, r_d), (fock, r_k))

    def p1_copy(m, d):
        tile, buf = gathers[m]
        slot_a = (y * 2 + zz) * 8
        slot_b = (8 + zz * 4 + y) * 8
        kind, off = d
        if kind == "a":
            return remote(tile, buf.at[pl.ds(slot_a, 8)], p1_send.at[m, off], p1_recv_a.at[m, zz], dev(x, h, y, (z + off) % 4))
        return remote(tile, buf.at[pl.ds(slot_b, 8)], p1_send.at[m, off], p1_recv_b.at[m, y], dev(x, h, (y + off) % 4, z))

    def p1_local_copy(m):
        tile, buf = gathers[m]
        slot = jnp.where(k == 0, y * 2 + zz, 8 + zz * 4 + y) * 8
        return pltpu.make_async_copy(tile, buf.at[pl.ds(slot, 8)], p1_local.at[m])

    def p1_start(m):
        for off in (1, 3, 2, 0):
            go = (k != h) if off == 0 else True

            @pl.when((k == 0) & go)
            def _():
                p1_copy(m, ("a", off)).start()

            @pl.when((k == 1) & go)
            def _():
                p1_copy(m, ("b", off)).start()

        @pl.when(k == h)
        def _():
            p1_local_copy(m).start()

    def p1_wait_send(m):
        for off in (1, 3, 2, 0):
            go = (k != h) if off == 0 else True

            @pl.when((k == 0) & go)
            def _():
                p1_copy(m, ("a", off)).wait_send()

            @pl.when((k == 1) & go)
            def _():
                p1_copy(m, ("b", off)).wait_send()

    def recv_wait(buf, start, n, sem):
        view = buf.at[pl.ds(start, n)]
        remote(view, view, sem, sem, dev(x, 1 - k, y, z)).wait_recv()

    def p1_wait(m):
        tile, buf = gathers[m]

        @pl.when(k == h)
        def _():
            p1_local_copy(m).wait()

        for q in range(2):
            mine = (k == 0) & (h == 0) & (zz == q)

            @pl.when(jnp.logical_not(mine))
            def _():
                recv_wait(buf, (y * 2 + q) * 8, 8, p1_recv_a.at[m, q])

        for yy in range(4):
            mine = (k == 1) & (y == yy)

            @pl.when((k == h) & jnp.logical_not(mine))
            def _():
                recv_wait(buf, (8 + zz * 4 + yy) * 8, 8, p1_recv_b.at[m, yy])

    def p2_a(m, src, half, off, fwd):
        buf = gathers[m][1]
        view = buf.at[pl.ds(src * 16 + half * 8, 8)]
        ssem = p2_send.at[m, 0, fwd * 4 + half * 2 + (off == 3)]
        return remote(view, view, ssem, p2_recv_a.at[m, src, half], dev(x, k, (y + off) % 4, z))

    def p2_b(m, q, half, off, fwd):
        buf = gathers[m][1]
        view = buf.at[pl.ds(64 + q * 32 + half * 16, 16)]
        ssem = p2_send.at[m, 1, fwd * 4 + half * 2 + (off == 3)]
        return remote(view, view, ssem, p2_recv_b.at[m, q, half], dev(x, k, y, (z + off) % 4))

    ways = ((0, 1), (1, 3), (1, 1), (0, 3))

    def p2_start(m):
        for half, off in ways:
            p2_a(m, y, half, off, 0).start()

            @pl.when(k == h)
            def _():
                p2_b(m, zz, half, off, 0).start()

    def p2_wait_a(m, src, half):
        recv_wait(gathers[m][1], src * 16 + half * 8, 8, p2_recv_a.at[m, src, half])

    def p2_wait_b(m, q, half):
        recv_wait(gathers[m][1], 64 + q * 32 + half * 16, 16, p2_recv_b.at[m, q, half])

    def near(off):
        return (z + 4 - off) % 4 // 2 == k

    def p2_relay(m):
        for half, off in ways[:2]:
            src = (y + 4 - off) % 4
            p2_wait_a(m, src, half)
            p2_a(m, src, half, off, 1).start()
            q = (z + 4 - off) % 2

            @pl.when(near(off))
            def _():
                p2_wait_b(m, q, half)
                p2_b(m, q, half, off, 1).start()

    def p2_wait(m):
        for half, off in ways[2:]:
            p2_wait_a(m, (y + 4 - off) % 4, half)
            q = (z + 4 - off) % 2

            @pl.when(near(off))
            def _():
                p2_wait_b(m, q, half)
        for half in range(2):
            p2_wait_a(m, (y + 2) % 4, half)

            @pl.when(near(2))
            def _():
                p2_wait_b(m, zz, half)

    def p2_wait_send(m):
        for half, off in ways:
            p2_a(m, y, half, off, 0).wait_send()

            @pl.when(k == h)
            def _():
                p2_b(m, zz, half, off, 0).wait_send()
        for half, off in ways[:2]:
            p2_a(m, (y + 4 - off) % 4, half, off, 1).wait_send()

            @pl.when(near(off))
            def _():
                p2_b(m, (z + 4 - off) % 2, half, off, 1).wait_send()

    def l_swap(n, src, buf):
        return remote(src, buf.at[k], l_send.at[n], l_recv.at[n], dev(x, 1 - k, y, z))

    l_swap(0, step, l_p).start()
    pltpu.make_async_copy(step, l_p.at[k], l_local.at[0]).start()
    p1_start(0)

    base = row * 4

    def make_pick(n, carry):
        i, t, s = n // 8, (n // 2) % 4, n % 2
        j = cols[base + i, (2 * t + k) * 2 + s]
        jj = jnp.maximum(j, 0)
        w, q = jj & 3, (jj >> 2) & 1
        for a in range(4):
            c = a // 2
            kk = cols[base + i, 4 * x + a]
            tile = t * 2 + q if c == 0 else 8 + q * 4 + t
            block = tile * 8 + w * 2
            live = (j >= 0) & (kk >= 0)
            first = cols[jj, 4 * x + 2 * c]
            second = cols[jj, 4 * x + 2 * c + 1]
            got = jnp.where(first == kk, block, jnp.where(second == kk, block + 1, ZERO))
            pick[n * 4 + a] = jnp.where(live, got, ZERO)
        return carry

    def make_tpick(n, carry):
        i, s = n // 2, n % 2
        j = cols[base + i, col * 2 + s]
        jj = jnp.maximum(j, 0)
        w, q = jj & 3, (jj >> 2) & 1
        block = q * 8 + w * 2
        g = (2 * y + h) * 2
        first = cols[jj, g]
        second = cols[jj, g + 1]
        got = jnp.where(first == base + i, block, jnp.where(second == base + i, block + 1, TZERO))
        tpick[n] = jnp.where(j >= 0, got, TZERO)
        return carry

    lax.fori_loop(0, 32, make_pick, 0)
    lax.fori_loop(0, 8, make_tpick, 0)

    p1_wait(0)
    p2_start(0)
    p1_start(1)
    p2_relay(0)

    def rs_copy(n, off):
        return remote(
            parts.at[n, (x + off) % 4], landed.at[n, off], rs_send.at[n, off], rs_recv.at[n, off],
            dev((x + off) % 4, k, y, z),
        )

    def stage(n, left, right):
        for off in (2, 1, 3, 0):
            t = (x + off) % 4

            def one_row(i, carry):
                lhs = jnp.concatenate([left[a // 2, i * 2 + a % 2] for a in range(4)], axis=1)
                rhs = jnp.concatenate(
                    [
                        jnp.concatenate([right[pick[((i * 4 + t) * 2 + s) * 4 + a]] for a in range(4)], axis=1)
                        for s in range(2)
                    ],
                    axis=0,
                )
                got = lax.dot_general(lhs, rhs, (((1,), (1,)), ((), ())), preferred_element_type=F32)
                for s in range(2):
                    block = got[:, s * 128 : (s + 1) * 128]
                    if off == 0:
                        own[n, i * 2 + s] = block
                    else:
                        parts[n, t, i * 2 + s] = block.astype(BF)
                return carry

            lax.fori_loop(0, 4, one_row, 0)
            if off != 0:
                rs_copy(n, off).start()

    def rs_wait(n):
        for off in (1, 3, 2):
            rs_copy(n, off).wait()

    def total(n, b):
        acc = own[n, b]
        for off in (1, 3, 2):
            acc = acc + landed[n, off, b].astype(F32)
        return acc

    def x_copy(n, q):
        return remote(
            x_send.at[n], x_recv[n].at[pl.ds(zz * 8, 8)], x_ssem.at[n, q], x_rsem.at[n, zz],
            dev(y, h, x, 2 * k + q),
        )

    def x_local_copy(n):
        return pltpu.make_async_copy(x_send.at[n], x_recv[n].at[pl.ds(zz * 8, 8)], x_local.at[n])

    def x_self(q):
        return (x == y) & (k == h) & (zz == q)

    def to_relay(n, c):
        return remote(
            x_send.at[n, pl.ds(c * 4, 4)], relay.at[n, y, pl.ds(c * 4, 4)], rl_ssem.at[n, c], rl_rsem.at[n, y, c],
            dev(x, k, x, z),
        )

    def from_relay(n, yy, c, q):
        return remote(
            relay.at[n, yy, pl.ds(c * 4, 4)], x_recv[n].at[pl.ds(zz * 8 + c * 4, 4)], rl_fsem.at[n, yy, c * 2 + q],
            x_rsem.at[n, zz], dev(yy, h, x, 2 * k + q),
        )

    by_relay = (k == 1) & (x != y)
    is_relay = (k == 1) & (x == y)

    def x_start(n):
        @pl.when(by_relay)
        def _():
            for c in range(2):
                to_relay(n, c).start()

        for q in range(2):
            @pl.when(jnp.logical_not(x_self(q) | by_relay))
            def _():
                x_copy(n, q).start()

            @pl.when(x_self(q))
            def _():
                x_local_copy(n).start()

    def x_relay(n):
        @pl.when(is_relay)
        def _():
            for c in range(2):
                for o in (1, 3, 2):
                    yy = (y + o) % 4
                    view = relay.at[n, yy, pl.ds(c * 4, 4)]
                    remote(view, view, rl_ssem.at[n, c], rl_rsem.at[n, yy, c], dev(x, 1 - k, y, z)).wait_recv()
                    for q in range(2):
                        from_relay(n, yy, c, q).start()

    def x_wait(n):
        for q in range(2):
            @pl.when(jnp.logical_not(x_self(q)))
            def _():
                recv_wait(x_recv[n], q * 8, 8, x_rsem.at[n, q])

            @pl.when(jnp.logical_not(x_self(q) | by_relay))
            def _():
                x_copy(n, q).wait_send()

            @pl.when(x_self(q))
            def _():
                x_local_copy(n).wait()

        @pl.when(by_relay)
        def _():
            for c in range(2):
                to_relay(n, c).wait_send()

        @pl.when(is_relay)
        def _():
            for c in range(2):
                for o in (1, 3, 2):
                    for q in range(2):
                        from_relay(n, (y + o) % 4, c, q).wait_send()

    def flipped(n, b):
        return x_recv[n][tpick[b]].astype(F32).T

    pltpu.make_async_copy(step, l_p.at[k], l_local.at[0]).wait()
    l_swap(0, step, l_p).wait()
    p2_wait(0)
    stage(0, l_p, r_i)
    p1_wait(1)
    p2_start(1)
    p1_start(2)
    rs_wait(0)

    def s_block(b, carry):
        l_s[k, b] = total(0, b).astype(BF)
        return carry

    lax.fori_loop(0, 8, s_block, 0)
    l_swap(1, l_s.at[k], l_s).start()
    p2_relay(1)
    p2_wait(1)
    l_swap(1, l_s.at[k], l_s).wait()

    stage(1, l_s, r_d)
    p1_wait(2)
    p2_start(2)
    rs_wait(1)

    def x_block(b, carry):
        v = total(1, b)
        own[1, b] = v
        x_send[0, b] = v.astype(BF)
        return carry

    lax.fori_loop(0, 8, x_block, 0)
    x_start(0)
    x_relay(0)
    p2_relay(2)
    x_wait(0)

    def c_block(b, acc):
        c = (-(own[1, b] + flipped(0, b))).astype(BF)
        l_c[k, b] = c
        prod = c.astype(F32) * fock[b].astype(F32)
        return acc + prod.reshape(16, 8, 128).sum(axis=0)

    tsum = lax.fori_loop(0, 8, c_block, jnp.zeros((8, 128), F32))
    l_swap(2, l_c.at[k], l_c).start()

    def t_copy(level, off):
        if level == 0:
            target, slot = (row, (col + off) % 8), col
        elif level == 1:
            target, slot = dev(x, k, (y + off) % 4, z), y
        else:
            target, slot = dev(x, k, y, (z + off) % 4), z
        return remote(t_src.at[level], t_buf.at[level, slot], t_send.at[level, off], t_recv.at[level, slot], target)

    sizes = (8, 4, 4)
    mine = (col, y, z)

    def t_start(level, value):
        t_src[level] = value
        for off in range(1, sizes[level]):
            t_copy(level, off).start()

    def t_finish(level, value):
        acc = jnp.zeros((8, 128), F32)
        for q in range(sizes[level]):
            @pl.when(mine[level] != q)
            def _():
                remote(
                    t_src.at[level], t_buf.at[level, q], t_recv.at[level, q], t_recv.at[level, q], dev(x, 1 - k, y, z)
                ).wait_recv()

        for off in range(1, sizes[level]):
            t_copy(level, off).wait_send()
        for q in range(sizes[level]):
            acc = acc + jnp.where(mine[level] == q, value, t_buf[level, q])
        return acc

    t_start(0, tsum)
    p2_wait(2)
    l_swap(2, l_c.at[k], l_c).wait()

    stage(2, l_c, r_k)
    tsum = t_finish(0, tsum)
    t_start(1, tsum)
    rs_wait(2)

    def w_block(b, carry):
        v = total(2, b)
        own[2, b] = v
        x_send[1, b] = v.astype(BF)
        return carry

    lax.fori_loop(0, 8, w_block, 0)
    x_start(1)
    x_relay(1)
    tsum = t_finish(1, tsum)
    t_start(2, tsum)
    for m in range(3):
        p1_wait_send(m)
        p2_wait_send(m)
    tsum = t_finish(2, tsum)
    trace[0, 0] = jnp.sum(tsum) * (1.0 / 1048576.0)
    x_wait(1)

    def o_block(b, carry):
        out[b] = (flipped(1, b) - own[2, b]).astype(BF)
        return carry

    lax.fori_loop(0, 8, o_block, 0)


def per_device(block_cols, step_dir, intersection, density, kohn_sham):
    flat = lambda a: a.reshape(8, 128, 128)
    vmem = pl.BlockSpec(memory_space=pltpu.VMEM)
    smem = pl.BlockSpec(memory_space=pltpu.SMEM)
    dma = pltpu.SemaphoreType.DMA
    blk = (128, 128)
    out, trace = pl.pallas_call(
        kernel,
        out_shape=(jax.ShapeDtypeStruct((8, 128, 128), BF), jax.ShapeDtypeStruct((1, 1), F32)),
        in_specs=[smem, vmem, vmem, vmem, vmem],
        out_specs=(vmem, smem),
        scratch_shapes=[
            pltpu.VMEM((129,) + blk, BF), pltpu.VMEM((129,) + blk, BF), pltpu.VMEM((129,) + blk, BF),
            pltpu.VMEM((2, 8) + blk, BF), pltpu.VMEM((2, 8) + blk, BF), pltpu.VMEM((2, 8) + blk, BF),
            pltpu.VMEM((3, 4, 8) + blk, BF), pltpu.VMEM((3, 4, 8) + blk, BF), pltpu.VMEM((3, 8) + blk, F32),
            pltpu.VMEM((2, 8) + blk, BF), pltpu.VMEM((17,) + blk, BF), pltpu.VMEM((17,) + blk, BF),
            pltpu.VMEM((3, 8, 128), F32), pltpu.VMEM((3, 8, 8, 128), F32),
            pltpu.SMEM((128,), jnp.int32), pltpu.SMEM((8,), jnp.int32),
            dma((3, 4)), dma((3, 2)), dma((3, 4)), dma((3,)), dma((3, 2, 8)), dma((3, 4, 2)), dma((3, 2, 2)),
            dma((3,)), dma((3,)), dma((1,)), dma((3, 4)), dma((3, 4)), dma((2, 2)), dma((2, 2)), dma((2,)),
            pltpu.VMEM((2, 4, 8) + blk, BF), dma((2, 2)), dma((2, 4, 2)), dma((2, 4, 4)),
            dma((3, 8)), dma((3, 8)),
        ],
        compiler_params=pltpu.CompilerParams(
            collective_id=0, has_side_effects=True, vmem_limit_bytes=48 * 2**20
        ),
        name="hessian",
    )(block_cols, flat(step_dir), flat(intersection), flat(density), flat(kohn_sham))
    return out.reshape(4, 2, 128, 128), trace.reshape(())


def solution(mesh):
    spec = P("row", "col", None, None)
    return jax.shard_map(
        per_device, mesh=mesh, in_specs=(P(), spec, spec, spec, spec), out_specs=(spec, P()), check_vma=False
    )
```

```python
import jax
import jax.numpy as jnp
from jax import lax
from jax.experimental import pallas as pl
from jax.experimental.pallas import tpu as pltpu
from jax.sharding import PartitionSpec as P

MESH = pl.DeviceIdType.MESH
BF = jnp.bfloat16
F32 = jnp.float32
ZERO = 128
TZERO = 16


def kernel(
    cols_hbm, step, inter, dens, fock_hbm, out, trace,
    cols, fock, in_sem,
    r_i, r_d, r_k, l_p, l_s, l_c, parts, landed, own, x_send, x_recv0, x_recv1, t_src, t_buf, pick, tpick,
    p1_send, p1_recv_a, p1_recv_b, p1_local, p2_send, p2_recv_a, p2_recv_b,
    l_send, l_recv, l_local, rs_send, rs_recv, x_ssem, x_rsem, x_local, relay, rl_ssem, rl_rsem, rl_fsem, t_send, t_recv,
):
    cols_copy = pltpu.make_async_copy(cols_hbm, cols, in_sem.at[0])
    cols_copy.start()
    fock_copy = pltpu.make_async_copy(fock_hbm, fock, in_sem.at[1])
    fock_copy.start()
    row = lax.axis_index("row")
    col = lax.axis_index("col")
    x, k = col // 2, col % 2
    y, z = row // 4, row % 4
    h = z // 2
    zz = z % 2

    x_recv = (x_recv0, x_recv1)

    def dev(x_, k_, y_, z_):
        return (y_ * 4 + z_, x_ * 2 + k_)

    def remote(src, dst, ssem, rsem, target):
        return pltpu.make_async_remote_copy(src, dst, ssem, rsem, device_id=target, device_id_type=MESH)

    barrier = pltpu.get_barrier_semaphore()
    for d in range(1, 8):
        pl.semaphore_signal(barrier, 1, device_id=(row, (col + d) % 8), device_id_type=MESH)
    for d in range(1, 4):
        for kk in range(2):
            pl.semaphore_signal(barrier, 1, device_id=dev(x, kk, (y + d) % 4, z), device_id_type=MESH)
            pl.semaphore_signal(barrier, 1, device_id=dev(x, kk, y, (z + d) % 4), device_id_type=MESH)
    for q in range(2):
        is_self = (x == y) & (k == h) & (zz == q)

        @pl.when(jnp.logical_not(is_self))
        def _():
            pl.semaphore_signal(barrier, 1, device_id=dev(y, h, x, 2 * k + q), device_id_type=MESH)

    for q in range(2):
        @pl.when((h == 1) & (x != y))
        def _():
            pl.semaphore_signal(barrier, 1, device_id=dev(y, 1, y, 2 * k + q), device_id_type=MESH)

    r_i[ZERO] = jnp.zeros((128, 128), BF)
    r_d[ZERO] = jnp.zeros((128, 128), BF)
    r_k[ZERO] = jnp.zeros((128, 128), BF)
    x_recv0[TZERO] = jnp.zeros((128, 128), BF)
    x_recv1[TZERO] = jnp.zeros((128, 128), BF)
    pl.semaphore_wait(barrier, 21 - jnp.where((x == y) & (k == h), 1, 0) + jnp.where((x == y) & (k == 1), 6, 0))

    gathers = ((inter, r_i), (dens, r_d), (fock_hbm, r_k))

    def p1_copy(m, d):
        tile, buf = gathers[m]
        slot_a = (y * 2 + zz) * 8
        slot_b = (8 + zz * 4 + y) * 8
        kind, off = d
        if kind == "a":
            return remote(tile, buf.at[pl.ds(slot_a, 8)], p1_send.at[m, off], p1_recv_a.at[m, zz], dev(x, h, y, (z + off) % 4))
        return remote(tile, buf.at[pl.ds(slot_b, 8)], p1_send.at[m, off], p1_recv_b.at[m, y], dev(x, h, (y + off) % 4, z))

    def p1_local_copy(m):
        tile, buf = gathers[m]
        slot = jnp.where(k == 0, y * 2 + zz, 8 + zz * 4 + y) * 8
        return pltpu.make_async_copy(tile, buf.at[pl.ds(slot, 8)], p1_local.at[m])

    def p1_start(m):
        for off in (1, 3, 2, 0):
            go = (k != h) if off == 0 else True

            @pl.when((k == 0) & go)
            def _():
                p1_copy(m, ("a", off)).start()

            @pl.when((k == 1) & go)
            def _():
                p1_copy(m, ("b", off)).start()

        @pl.when(k == h)
        def _():
            p1_local_copy(m).start()

    def p1_wait_send(m):
        for off in (1, 3, 2, 0):
            go = (k != h) if off == 0 else True

            @pl.when((k == 0) & go)
            def _():
                p1_copy(m, ("a", off)).wait_send()

            @pl.when((k == 1) & go)
            def _():
                p1_copy(m, ("b", off)).wait_send()

    def recv_wait(buf, start, n, sem):
        view = buf.at[pl.ds(start, n)]
        remote(view, view, sem, sem, dev(x, 1 - k, y, z)).wait_recv()

    def p1_wait(m):
        tile, buf = gathers[m]

        @pl.when(k == h)
        def _():
            p1_local_copy(m).wait()

        for q in range(2):
            mine = (k == 0) & (h == 0) & (zz == q)

            @pl.when(jnp.logical_not(mine))
            def _():
                recv_wait(buf, (y * 2 + q) * 8, 8, p1_recv_a.at[m, q])

        for yy in range(4):
            mine = (k == 1) & (y == yy)

            @pl.when((k == h) & jnp.logical_not(mine))
            def _():
                recv_wait(buf, (8 + zz * 4 + yy) * 8, 8, p1_recv_b.at[m, yy])

    def p2_a(m, src, half, off, fwd):
        buf = gathers[m][1]
        view = buf.at[pl.ds(src * 16 + half * 8, 8)]
        ssem = p2_send.at[m, 0, fwd * 4 + half * 2 + (off == 3)]
        return remote(view, view, ssem, p2_recv_a.at[m, src, half], dev(x, k, (y + off) % 4, z))

    def p2_b(m, q, half, off, fwd):
        buf = gathers[m][1]
        view = buf.at[pl.ds(64 + q * 32 + half * 16, 16)]
        ssem = p2_send.at[m, 1, fwd * 4 + half * 2 + (off == 3)]
        return remote(view, view, ssem, p2_recv_b.at[m, q, half], dev(x, k, y, (z + off) % 4))

    ways = ((0, 1), (1, 3), (1, 1), (0, 3))

    def p2_start(m):
        for half, off in ways:
            p2_a(m, y, half, off, 0).start()

            @pl.when(k == h)
            def _():
                p2_b(m, zz, half, off, 0).start()

    def p2_wait_a(m, src, half):
        recv_wait(gathers[m][1], src * 16 + half * 8, 8, p2_recv_a.at[m, src, half])

    def p2_wait_b(m, q, half):
        recv_wait(gathers[m][1], 64 + q * 32 + half * 16, 16, p2_recv_b.at[m, q, half])

    def near(off):
        return (z + 4 - off) % 4 // 2 == k

    def p2_relay(m):
        for half, off in ways[:2]:
            src = (y + 4 - off) % 4
            p2_wait_a(m, src, half)
            p2_a(m, src, half, off, 1).start()
            q = (z + 4 - off) % 2

            @pl.when(near(off))
            def _():
                p2_wait_b(m, q, half)
                p2_b(m, q, half, off, 1).start()

    def p2_wait(m):
        for half, off in ways[2:]:
            p2_wait_a(m, (y + 4 - off) % 4, half)
            q = (z + 4 - off) % 2

            @pl.when(near(off))
            def _():
                p2_wait_b(m, q, half)
        for half in range(2):
            p2_wait_a(m, (y + 2) % 4, half)

            @pl.when(near(2))
            def _():
                p2_wait_b(m, zz, half)

    def p2_wait_send(m):
        for half, off in ways:
            p2_a(m, y, half, off, 0).wait_send()

            @pl.when(k == h)
            def _():
                p2_b(m, zz, half, off, 0).wait_send()
        for half, off in ways[:2]:
            p2_a(m, (y + 4 - off) % 4, half, off, 1).wait_send()

            @pl.when(near(off))
            def _():
                p2_b(m, (z + 4 - off) % 2, half, off, 1).wait_send()

    def l_swap(n, src, buf, c):
        part = pl.ds(c * 4, 4)
        return remote(src.at[part], buf.at[k, part], l_send.at[n, c], l_recv.at[n, c], dev(x, 1 - k, y, z))

    def l_wait(n, src, buf):
        for c in range(2):
            l_swap(n, src, buf, c).wait()

    pltpu.make_async_copy(step, l_p.at[k], l_local.at[0]).start()
    p1_start(0)
    for c in range(2):
        l_swap(0, step, l_p, c).start()
    p1_start(1)

    base = row * 4

    def make_pick(n, carry):
        i, t, s = n // 8, (n // 2) % 4, n % 2
        j = cols[base + i, (2 * t + k) * 2 + s]
        jj = jnp.maximum(j, 0)
        w, q = jj & 3, (jj >> 2) & 1
        for a in range(4):
            c = a // 2
            kk = cols[base + i, 4 * x + a]
            tile = t * 2 + q if c == 0 else 8 + q * 4 + t
            block = tile * 8 + w * 2
            live = (j >= 0) & (kk >= 0)
            first = cols[jj, 4 * x + 2 * c]
            second = cols[jj, 4 * x + 2 * c + 1]
            got = jnp.where(first == kk, block, jnp.where(second == kk, block + 1, ZERO))
            pick[n * 4 + a] = jnp.where(live, got, ZERO)
        return carry

    def make_tpick(n, carry):
        i, s = n // 2, n % 2
        j = cols[base + i, col * 2 + s]
        jj = jnp.maximum(j, 0)
        w, q = jj & 3, (jj >> 2) & 1
        block = q * 8 + w * 2
        g = (2 * y + h) * 2
        first = cols[jj, g]
        second = cols[jj, g + 1]
        got = jnp.where(first == base + i, block, jnp.where(second == base + i, block + 1, TZERO))
        tpick[n] = jnp.where(j >= 0, got, TZERO)
        return carry

    cols_copy.wait()
    fock_copy.wait()
    lax.fori_loop(0, 32, make_pick, 0)
    lax.fori_loop(0, 8, make_tpick, 0)

    p1_wait(0)
    p2_start(0)
    p2_relay(0)
    p1_wait(1)
    p2_start(1)

    def rs_copy(n, off, c):
        part = pl.ds(c * 4, 4)
        return remote(
            parts.at[n, (x + off) % 4, part], landed.at[n, off, part], rs_send.at[n, off, c], rs_recv.at[n, off, c],
            dev((x + off) % 4, k, y, z),
        )

    def stage(n, left, right):
        def rows(off, lo, hi):
            t = (x + off) % 4

            def one_row(i, carry):
                lhs = jnp.concatenate([left[a // 2, i * 2 + a % 2] for a in range(4)], axis=1)
                rhs = jnp.concatenate(
                    [
                        jnp.concatenate([right[pick[((i * 4 + t) * 2 + s) * 4 + a]] for a in range(4)], axis=1)
                        for s in range(2)
                    ],
                    axis=0,
                )
                got = lax.dot_general(lhs, rhs, (((1,), (1,)), ((), ())), preferred_element_type=F32)
                for s in range(2):
                    block = got[:, s * 128 : (s + 1) * 128]
                    if off == 0:
                        own[n, i * 2 + s] = block
                    else:
                        parts[n, t, i * 2 + s] = block.astype(BF)
                return carry

            lax.fori_loop(lo, hi, one_row, 0)

        for c in range(2):
            for off in (2, 1, 3):
                rows(off, c * 2, c * 2 + 2)
                rs_copy(n, off, c).start()
        rows(0, 0, 4)

    def rs_wait(n, c):
        for off in (1, 3, 2):
            rs_copy(n, off, c).wait()

    def total(n, b):
        acc = own[n, b]
        for off in (1, 3, 2):
            acc = acc + landed[n, off, b].astype(F32)
        return acc

    def x_copy(n, q, c):
        return remote(
            x_send.at[n, pl.ds(c * 4, 4)], x_recv[n].at[pl.ds(zz * 8 + c * 4, 4)], x_ssem.at[n, q, c],
            x_rsem.at[n, zz], dev(y, h, x, 2 * k + q),
        )

    def x_local_copy(n, c):
        return pltpu.make_async_copy(
            x_send.at[n, pl.ds(c * 4, 4)], x_recv[n].at[pl.ds(zz * 8 + c * 4, 4)], x_local.at[n, c]
        )

    def x_self(q):
        return (x == y) & (k == h) & (zz == q)

    def to_relay(n, c):
        return remote(
            x_send.at[n, pl.ds(c * 4, 4)], relay.at[n, y, pl.ds(c * 4, 4)], rl_ssem.at[n, c], rl_rsem.at[n, y, c],
            dev(x, k, x, z),
        )

    def from_relay(n, yy, c, q):
        return remote(
            relay.at[n, yy, pl.ds(c * 4, 4)], x_recv[n].at[pl.ds(zz * 8 + c * 4, 4)], rl_fsem.at[n, yy, c * 2 + q],
            x_rsem.at[n, zz], dev(yy, h, x, 2 * k + q),
        )

    by_relay = (k == 1) & (x != y)
    is_relay = (k == 1) & (x == y)

    def x_start(n, c):
        @pl.when(by_relay)
        def _():
            to_relay(n, c).start()

        for q in range(2):
            @pl.when(jnp.logical_not(x_self(q) | by_relay))
            def _():
                x_copy(n, q, c).start()

            @pl.when(x_self(q))
            def _():
                x_local_copy(n, c).start()

    def x_relay(n, c):
        @pl.when(is_relay)
        def _():
            for o in (1, 3, 2):
                yy = (y + o) % 4
                view = relay.at[n, yy, pl.ds(c * 4, 4)]
                remote(view, view, rl_ssem.at[n, c], rl_rsem.at[n, yy, c], dev(x, 1 - k, y, z)).wait_recv()
                for q in range(2):
                    from_relay(n, yy, c, q).start()

    def x_wait(n):
        for q in range(2):
            @pl.when(jnp.logical_not(x_self(q)))
            def _():
                recv_wait(x_recv[n], q * 8, 8, x_rsem.at[n, q])

            @pl.when(x_self(q))
            def _():
                for c in range(2):
                    x_local_copy(n, c).wait()

    def x_wait_send(n):
        for c in range(2):
            for q in range(2):
                @pl.when(jnp.logical_not(x_self(q) | by_relay))
                def _():
                    x_copy(n, q, c).wait_send()

            @pl.when(by_relay)
            def _():
                to_relay(n, c).wait_send()

            @pl.when(is_relay)
            def _():
                for o in (1, 3, 2):
                    for q in range(2):
                        from_relay(n, (y + o) % 4, c, q).wait_send()

    def flipped(n, b):
        return x_recv[n][tpick[b]].astype(F32).T

    pltpu.make_async_copy(step, l_p.at[k], l_local.at[0]).wait()
    l_wait(0, step, l_p)
    p2_wait(0)
    stage(0, l_p, r_i)

    def s_block(b, carry):
        l_s[k, b] = total(0, b).astype(BF)
        return carry

    for c in range(2):
        rs_wait(0, c)
        lax.fori_loop(c * 4, c * 4 + 4, s_block, 0)
        l_swap(1, l_s.at[k], l_s, c).start()
        if c == 0:
            p2_relay(1)
            p1_start(2)
    l_wait(1, l_s.at[k], l_s)
    p2_wait(1)

    stage(1, l_s, r_d)

    def x_block(b, carry):
        v = total(1, b)
        own[1, b] = v
        x_send[0, b] = v.astype(BF)
        return carry

    for c in range(2):
        rs_wait(1, c)
        lax.fori_loop(c * 4, c * 4 + 4, x_block, 0)
        x_start(0, c)
        if c == 0:
            p1_wait(2)
            p2_start(2)
    x_relay(0, 0)
    x_relay(0, 1)
    p2_relay(2)
    x_wait(0)

    def c_block(b, acc):
        c = (-(own[1, b] + flipped(0, b))).astype(BF)
        l_c[k, b] = c
        prod = c.astype(F32) * fock[b].astype(F32)
        return acc + prod.reshape(16, 8, 128).sum(axis=0)

    tsum = jnp.zeros((8, 128), F32)
    for c in range(2):
        tsum = lax.fori_loop(c * 4, c * 4 + 4, c_block, tsum)
        l_swap(2, l_c.at[k], l_c, c).start()

    def t_copy(level, off):
        if level == 0:
            target, slot = (row, (col + off) % 8), col
        elif level == 1:
            target, slot = dev(x, k, (y + off) % 4, z), y
        else:
            target, slot = dev(x, k, y, (z + off) % 4), z
        return remote(t_src.at[level], t_buf.at[level, slot], t_send.at[level, off], t_recv.at[level, slot], target)

    sizes = (8, 4, 4)
    mine = (col, y, z)

    def t_start(level, value):
        t_src[level] = value
        for off in range(1, sizes[level]):
            t_copy(level, off).start()

    def t_finish(level, value):
        acc = jnp.zeros((8, 128), F32)
        for q in range(sizes[level]):
            @pl.when(mine[level] != q)
            def _():
                remote(
                    t_src.at[level], t_buf.at[level, q], t_recv.at[level, q], t_recv.at[level, q], dev(x, 1 - k, y, z)
                ).wait_recv()

        for off in range(1, sizes[level]):
            t_copy(level, off).wait_send()
        for q in range(sizes[level]):
            acc = acc + jnp.where(mine[level] == q, value, t_buf[level, q])
        return acc

    t_start(0, tsum)
    p2_wait(2)
    l_wait(2, l_c.at[k], l_c)

    stage(2, l_c, r_k)
    tsum = t_finish(0, tsum)
    t_start(1, tsum)

    def w_block(b, carry):
        v = total(2, b)
        own[2, b] = v
        x_send[1, b] = v.astype(BF)
        return carry

    for c in range(2):
        rs_wait(2, c)
        lax.fori_loop(c * 4, c * 4 + 4, w_block, 0)
        x_start(1, c)
    x_relay(1, 0)
    x_relay(1, 1)
    tsum = t_finish(1, tsum)
    t_start(2, tsum)
    for m in range(3):
        p1_wait_send(m)
        p2_wait_send(m)
    tsum = t_finish(2, tsum)
    trace[0, 0] = jnp.sum(tsum) * (1.0 / 1048576.0)
    x_wait(1)
    x_wait_send(0)
    x_wait_send(1)

    def o_block(b, carry):
        out[b] = (flipped(1, b) - own[2, b]).astype(BF)
        return carry

    lax.fori_loop(0, 8, o_block, 0)


def per_device(block_cols, step_dir, intersection, density, kohn_sham):
    flat = lambda a: a.reshape(8, 128, 128)
    vmem = pl.BlockSpec(memory_space=pltpu.VMEM)
    smem = pl.BlockSpec(memory_space=pltpu.SMEM)
    hbm = pl.BlockSpec(memory_space=pl.ANY)
    dma = pltpu.SemaphoreType.DMA
    blk = (128, 128)
    out, trace = pl.pallas_call(
        kernel,
        out_shape=(jax.ShapeDtypeStruct((8, 128, 128), BF), jax.ShapeDtypeStruct((1, 1), F32)),
        in_specs=[hbm] * 5,
        out_specs=(vmem, smem),
        scratch_shapes=[
            pltpu.SMEM((64, 16), jnp.int32), pltpu.VMEM((8,) + blk, BF), dma((2,)),
            pltpu.VMEM((129,) + blk, BF), pltpu.VMEM((129,) + blk, BF), pltpu.VMEM((129,) + blk, BF),
            pltpu.VMEM((2, 8) + blk, BF), pltpu.VMEM((2, 8) + blk, BF), pltpu.VMEM((2, 8) + blk, BF),
            pltpu.VMEM((3, 4, 8) + blk, BF), pltpu.VMEM((3, 4, 8) + blk, BF), pltpu.VMEM((3, 8) + blk, F32),
            pltpu.VMEM((2, 8) + blk, BF), pltpu.VMEM((17,) + blk, BF), pltpu.VMEM((17,) + blk, BF),
            pltpu.VMEM((3, 8, 128), F32), pltpu.VMEM((3, 8, 8, 128), F32),
            pltpu.SMEM((128,), jnp.int32), pltpu.SMEM((8,), jnp.int32),
            dma((3, 4)), dma((3, 2)), dma((3, 4)), dma((3,)), dma((3, 2, 8)), dma((3, 4, 2)), dma((3, 2, 2)),
            dma((3, 2)), dma((3, 2)), dma((1,)), dma((3, 4, 2)), dma((3, 4, 2)), dma((2, 2, 2)), dma((2, 2)), dma((2, 2)),
            pltpu.VMEM((2, 4, 8) + blk, BF), dma((2, 2)), dma((2, 4, 2)), dma((2, 4, 4)),
            dma((3, 8)), dma((3, 8)),
        ],
        compiler_params=pltpu.CompilerParams(
            collective_id=0, has_side_effects=True, vmem_limit_bytes=63_900_000
        ),
        name="hessian",
    )(block_cols, flat(step_dir), flat(intersection), flat(density), flat(kohn_sham))
    return out.reshape(4, 2, 128, 128), trace.reshape(())


def solution(mesh):
    spec = P("row", "col", None, None)
    return jax.shard_map(
        per_device, mesh=mesh, in_specs=(P(), spec, spec, spec, spec), out_specs=(spec, P()), check_vma=False
    )
```

```python
import jax
import jax.numpy as jnp
from jax import lax
from jax.experimental import pallas as pl
from jax.experimental.pallas import tpu as pltpu
from jax.sharding import PartitionSpec as P

MESH = pl.DeviceIdType.MESH
BF = jnp.bfloat16
F32 = jnp.float32
ZERO = 128
TZERO = 16


def kernel(
    cols_hbm, step, inter, dens, fock_hbm, out, trace,
    cols, fock, in_sem,
    r_i, r_d, r_k, l_p, l_s, l_c, parts, landed, own, x_send, x_recv0, x_recv1, t_src, t_buf, pick, tpick,
    p1_send, p1_recv_a, p1_recv_b, p1_local, p2_send, p2_recv_a, p2_recv_b,
    l_send, l_recv, l_local, rs_send, rs_recv, x_ssem, x_rsem, x_local, relay, rl_ssem, rl_rsem, rl_fsem, t_send, t_recv,
):
    cols_copy = pltpu.make_async_copy(cols_hbm, cols, in_sem.at[0])
    cols_copy.start()
    fock_copy = pltpu.make_async_copy(fock_hbm, fock, in_sem.at[1])
    fock_copy.start()
    row = lax.axis_index("row")
    col = lax.axis_index("col")
    x, k = col // 2, col % 2
    y, z = row // 4, row % 4
    h = z // 2
    zz = z % 2

    x_recv = (x_recv0, x_recv1)

    def dev(x_, k_, y_, z_):
        return (y_ * 4 + z_, x_ * 2 + k_)

    def remote(src, dst, ssem, rsem, target):
        return pltpu.make_async_remote_copy(src, dst, ssem, rsem, device_id=target, device_id_type=MESH)

    barrier = pltpu.get_barrier_semaphore()
    for d in range(1, 8):
        pl.semaphore_signal(barrier, 1, device_id=(row, (col + d) % 8), device_id_type=MESH)
    for d in range(1, 4):
        for kk in range(2):
            pl.semaphore_signal(barrier, 1, device_id=dev(x, kk, (y + d) % 4, z), device_id_type=MESH)
            pl.semaphore_signal(barrier, 1, device_id=dev(x, kk, y, (z + d) % 4), device_id_type=MESH)
    for q in range(2):
        is_self = (x == y) & (k == h) & (zz == q)

        @pl.when(jnp.logical_not(is_self))
        def _():
            pl.semaphore_signal(barrier, 1, device_id=dev(y, h, x, 2 * k + q), device_id_type=MESH)

    for q in range(2):
        @pl.when((h == 1) & (x != y))
        def _():
            pl.semaphore_signal(barrier, 1, device_id=dev(y, 1, y, 2 * k + q), device_id_type=MESH)

    r_i[ZERO] = jnp.zeros((128, 128), BF)
    r_d[ZERO] = jnp.zeros((128, 128), BF)
    r_k[ZERO] = jnp.zeros((128, 128), BF)
    x_recv0[TZERO] = jnp.zeros((128, 128), BF)
    x_recv1[TZERO] = jnp.zeros((128, 128), BF)
    pl.semaphore_wait(barrier, 21 - jnp.where((x == y) & (k == h), 1, 0) + jnp.where((x == y) & (k == 1), 6, 0))

    gathers = ((inter, r_i), (dens, r_d), (fock_hbm, r_k))

    def p1_copy(m, d):
        tile, buf = gathers[m]
        slot_a = (y * 2 + zz) * 8
        slot_b = (8 + zz * 4 + y) * 8
        kind, off = d
        if kind == "a":
            return remote(tile, buf.at[pl.ds(slot_a, 8)], p1_send.at[m, off], p1_recv_a.at[m, zz], dev(x, h, y, (z + off) % 4))
        return remote(tile, buf.at[pl.ds(slot_b, 8)], p1_send.at[m, off], p1_recv_b.at[m, y], dev(x, h, (y + off) % 4, z))

    def p1_local_copy(m):
        tile, buf = gathers[m]
        slot = jnp.where(k == 0, y * 2 + zz, 8 + zz * 4 + y) * 8
        return pltpu.make_async_copy(tile, buf.at[pl.ds(slot, 8)], p1_local.at[m])

    def p1_start(m):
        for off in (1, 3, 2, 0):
            go = (k != h) if off == 0 else True

            @pl.when((k == 0) & go)
            def _():
                p1_copy(m, ("a", off)).start()

            @pl.when((k == 1) & go)
            def _():
                p1_copy(m, ("b", off)).start()

        @pl.when(k == h)
        def _():
            p1_local_copy(m).start()

    def p1_wait_send(m):
        for off in (1, 3, 2, 0):
            go = (k != h) if off == 0 else True

            @pl.when((k == 0) & go)
            def _():
                p1_copy(m, ("a", off)).wait_send()

            @pl.when((k == 1) & go)
            def _():
                p1_copy(m, ("b", off)).wait_send()

    def recv_wait(buf, start, n, sem):
        view = buf.at[pl.ds(start, n)]
        remote(view, view, sem, sem, dev(x, 1 - k, y, z)).wait_recv()

    def p1_wait(m):
        tile, buf = gathers[m]

        @pl.when(k == h)
        def _():
            p1_local_copy(m).wait()

        for q in range(2):
            mine = (k == 0) & (h == 0) & (zz == q)

            @pl.when(jnp.logical_not(mine))
            def _():
                recv_wait(buf, (y * 2 + q) * 8, 8, p1_recv_a.at[m, q])

        for yy in range(4):
            mine = (k == 1) & (y == yy)

            @pl.when((k == h) & jnp.logical_not(mine))
            def _():
                recv_wait(buf, (8 + zz * 4 + yy) * 8, 8, p1_recv_b.at[m, yy])

    def p2_a(m, src, half, off, fwd):
        buf = gathers[m][1]
        view = buf.at[pl.ds(src * 16 + half * 8, 8)]
        ssem = p2_send.at[m, 0, fwd * 4 + half * 2 + (off == 3)]
        return remote(view, view, ssem, p2_recv_a.at[m, src, half], dev(x, k, (y + off) % 4, z))

    def p2_b(m, q, half, off, fwd):
        buf = gathers[m][1]
        view = buf.at[pl.ds(64 + q * 32 + half * 16, 16)]
        ssem = p2_send.at[m, 1, fwd * 4 + half * 2 + (off == 3)]
        return remote(view, view, ssem, p2_recv_b.at[m, q, half], dev(x, k, y, (z + off) % 4))

    ways = ((0, 1), (1, 3), (1, 1), (0, 3))

    def p2_start(m):
        for half, off in ways:
            p2_a(m, y, half, off, 0).start()

            @pl.when(k == h)
            def _():
                p2_b(m, zz, half, off, 0).start()

    def p2_wait_a(m, src, half):
        recv_wait(gathers[m][1], src * 16 + half * 8, 8, p2_recv_a.at[m, src, half])

    def p2_wait_b(m, q, half):
        recv_wait(gathers[m][1], 64 + q * 32 + half * 16, 16, p2_recv_b.at[m, q, half])

    def near(off):
        return (z + 4 - off) % 4 // 2 == k

    def p2_relay(m):
        for half, off in ways[:2]:
            src = (y + 4 - off) % 4
            p2_wait_a(m, src, half)
            p2_a(m, src, half, off, 1).start()
            q = (z + 4 - off) % 2

            @pl.when(near(off))
            def _():
                p2_wait_b(m, q, half)
                p2_b(m, q, half, off, 1).start()

    def p2_wait(m):
        for half, off in ways[2:]:
            p2_wait_a(m, (y + 4 - off) % 4, half)
            q = (z + 4 - off) % 2

            @pl.when(near(off))
            def _():
                p2_wait_b(m, q, half)
        for half in range(2):
            p2_wait_a(m, (y + 2) % 4, half)

            @pl.when(near(2))
            def _():
                p2_wait_b(m, zz, half)

    def p2_wait_send(m):
        for half, off in ways:
            p2_a(m, y, half, off, 0).wait_send()

            @pl.when(k == h)
            def _():
                p2_b(m, zz, half, off, 0).wait_send()
        for half, off in ways[:2]:
            p2_a(m, (y + 4 - off) % 4, half, off, 1).wait_send()

            @pl.when(near(off))
            def _():
                p2_b(m, (z + 4 - off) % 2, half, off, 1).wait_send()

    def l_swap(n, src, buf, c):
        part = pl.ds(c * 4, 4)
        return remote(src.at[part], buf.at[k, part], l_send.at[n, c], l_recv.at[n, c], dev(x, 1 - k, y, z))

    def l_wait(n, src, buf):
        for c in range(2):
            l_swap(n, src, buf, c).wait()

    pltpu.make_async_copy(step, l_p.at[k], l_local.at[0]).start()
    p1_start(0)
    for c in range(2):
        l_swap(0, step, l_p, c).start()
    p1_start(1)

    base = row * 4

    def make_pick(n, carry):
        i, t, s = n // 8, (n // 2) % 4, n % 2
        j = cols[(2 * t + k) * 2 + s, base + i]
        jj = jnp.maximum(j, 0)
        w, q = jj & 3, (jj >> 2) & 1
        for a in range(4):
            c = a // 2
            kk = cols[4 * x + a, base + i]
            tile = t * 2 + q if c == 0 else 8 + q * 4 + t
            block = tile * 8 + w * 2
            live = (j >= 0) & (kk >= 0)
            first = cols[4 * x + 2 * c, jj]
            second = cols[4 * x + 2 * c + 1, jj]
            got = jnp.where(first == kk, block, jnp.where(second == kk, block + 1, ZERO))
            pick[n * 4 + a] = jnp.where(live, got, ZERO)
        return carry

    def make_tpick(n, carry):
        i, s = n // 2, n % 2
        j = cols[col * 2 + s, base + i]
        jj = jnp.maximum(j, 0)
        w, q = jj & 3, (jj >> 2) & 1
        block = q * 8 + w * 2
        g = (2 * y + h) * 2
        first = cols[g, jj]
        second = cols[g + 1, jj]
        got = jnp.where(first == base + i, block, jnp.where(second == base + i, block + 1, TZERO))
        tpick[n] = jnp.where(j >= 0, got, TZERO)
        return carry

    cols_copy.wait()
    fock_copy.wait()
    lax.fori_loop(0, 32, make_pick, 0)
    lax.fori_loop(0, 8, make_tpick, 0)

    p1_wait(0)
    p2_start(0)
    p2_relay(0)
    p1_wait(1)
    p2_start(1)

    def rs_copy(n, off, c):
        part = pl.ds(c * 4, 4)
        return remote(
            parts.at[n, (x + off) % 4, part], landed.at[n, off, part], rs_send.at[n, off, c], rs_recv.at[n, off, c],
            dev((x + off) % 4, k, y, z),
        )

    def stage(n, left, right):
        def rows(off, lo, hi):
            t = (x + off) % 4

            def one_row(i, carry):
                lhs = jnp.concatenate([left[a // 2, i * 2 + a % 2] for a in range(4)], axis=1)
                rhs = jnp.concatenate(
                    [
                        jnp.concatenate([right[pick[((i * 4 + t) * 2 + s) * 4 + a]] for a in range(4)], axis=1)
                        for s in range(2)
                    ],
                    axis=0,
                )
                got = lax.dot_general(lhs, rhs, (((1,), (1,)), ((), ())), preferred_element_type=F32)
                for s in range(2):
                    block = got[:, s * 128 : (s + 1) * 128]
                    if off == 0:
                        own[n, i * 2 + s] = block
                    else:
                        parts[n, t, i * 2 + s] = block.astype(BF)
                return carry

            lax.fori_loop(lo, hi, one_row, 0)

        for c in range(2):
            for off in (2, 1, 3):
                rows(off, c * 2, c * 2 + 2)
                rs_copy(n, off, c).start()
        rows(0, 0, 4)

    def rs_wait(n, c):
        for off in (1, 3, 2):
            rs_copy(n, off, c).wait()

    def total(n, b):
        acc = own[n, b]
        for off in (1, 3, 2):
            acc = acc + landed[n, off, b].astype(F32)
        return acc

    def x_copy(n, q, c):
        return remote(
            x_send.at[n, pl.ds(c * 4, 4)], x_recv[n].at[pl.ds(zz * 8 + c * 4, 4)], x_ssem.at[n, q, c],
            x_rsem.at[n, zz], dev(y, h, x, 2 * k + q),
        )

    def x_local_copy(n, c):
        return pltpu.make_async_copy(
            x_send.at[n, pl.ds(c * 4, 4)], x_recv[n].at[pl.ds(zz * 8 + c * 4, 4)], x_local.at[n, c]
        )

    def x_self(q):
        return (x == y) & (k == h) & (zz == q)

    def to_relay(n, c):
        return remote(
            x_send.at[n, pl.ds(c * 4, 4)], relay.at[n, y, pl.ds(c * 4, 4)], rl_ssem.at[n, c], rl_rsem.at[n, y, c],
            dev(x, k, x, z),
        )

    def from_relay(n, yy, c, q):
        return remote(
            relay.at[n, yy, pl.ds(c * 4, 4)], x_recv[n].at[pl.ds(zz * 8 + c * 4, 4)], rl_fsem.at[n, yy, c * 2 + q],
            x_rsem.at[n, zz], dev(yy, h, x, 2 * k + q),
        )

    by_relay = (k == 1) & (x != y)
    is_relay = (k == 1) & (x == y)

    def x_start(n, c):
        @pl.when(by_relay)
        def _():
            to_relay(n, c).start()

        for q in range(2):
            @pl.when(jnp.logical_not(x_self(q) | by_relay))
            def _():
                x_copy(n, q, c).start()

            @pl.when(x_self(q))
            def _():
                x_local_copy(n, c).start()

    def x_relay(n, c):
        @pl.when(is_relay)
        def _():
            for o in (1, 3, 2):
                yy = (y + o) % 4
                view = relay.at[n, yy, pl.ds(c * 4, 4)]
                remote(view, view, rl_ssem.at[n, c], rl_rsem.at[n, yy, c], dev(x, 1 - k, y, z)).wait_recv()
                for q in range(2):
                    from_relay(n, yy, c, q).start()

    def x_wait(n):
        for q in range(2):
            @pl.when(jnp.logical_not(x_self(q)))
            def _():
                recv_wait(x_recv[n], q * 8, 8, x_rsem.at[n, q])

            @pl.when(x_self(q))
            def _():
                for c in range(2):
                    x_local_copy(n, c).wait()

    def x_wait_send(n):
        for c in range(2):
            for q in range(2):
                @pl.when(jnp.logical_not(x_self(q) | by_relay))
                def _():
                    x_copy(n, q, c).wait_send()

            @pl.when(by_relay)
            def _():
                to_relay(n, c).wait_send()

            @pl.when(is_relay)
            def _():
                for o in (1, 3, 2):
                    for q in range(2):
                        from_relay(n, (y + o) % 4, c, q).wait_send()

    def flipped(n, b):
        return x_recv[n][tpick[b]].astype(F32).T

    pltpu.make_async_copy(step, l_p.at[k], l_local.at[0]).wait()
    l_wait(0, step, l_p)
    p2_wait(0)
    stage(0, l_p, r_i)

    def s_block(b, carry):
        l_s[k, b] = total(0, b).astype(BF)
        return carry

    for c in range(2):
        rs_wait(0, c)
        lax.fori_loop(c * 4, c * 4 + 4, s_block, 0)
        l_swap(1, l_s.at[k], l_s, c).start()
        if c == 0:
            p2_relay(1)
            p1_start(2)
    l_wait(1, l_s.at[k], l_s)
    p2_wait(1)

    stage(1, l_s, r_d)

    def x_block(b, carry):
        v = total(1, b)
        own[1, b] = v
        x_send[0, b] = v.astype(BF)
        return carry

    for c in range(2):
        rs_wait(1, c)
        lax.fori_loop(c * 4, c * 4 + 4, x_block, 0)
        x_start(0, c)
        if c == 0:
            p1_wait(2)
            p2_start(2)
    x_relay(0, 0)
    x_relay(0, 1)
    p2_relay(2)
    x_wait(0)

    def c_block(b, acc):
        c = (-(own[1, b] + flipped(0, b))).astype(BF)
        l_c[k, b] = c
        prod = c.astype(F32) * fock[b].astype(F32)
        return acc + prod.reshape(16, 8, 128).sum(axis=0)

    tsum = jnp.zeros((8, 128), F32)
    for c in range(2):
        tsum = lax.fori_loop(c * 4, c * 4 + 4, c_block, tsum)
        l_swap(2, l_c.at[k], l_c, c).start()

    def t_copy(level, off):
        if level == 0:
            target, slot = (row, (col + off) % 8), col
        elif level == 1:
            target, slot = dev(x, k, (y + off) % 4, z), y
        else:
            target, slot = dev(x, k, y, (z + off) % 4), z
        return remote(t_src.at[level], t_buf.at[level, slot], t_send.at[level, off], t_recv.at[level, slot], target)

    sizes = (8, 4, 4)
    mine = (col, y, z)

    def t_start(level, value):
        t_src[level] = value
        for off in range(1, sizes[level]):
            t_copy(level, off).start()

    def t_finish(level, value):
        acc = jnp.zeros((8, 128), F32)
        for q in range(sizes[level]):
            @pl.when(mine[level] != q)
            def _():
                remote(
                    t_src.at[level], t_buf.at[level, q], t_recv.at[level, q], t_recv.at[level, q], dev(x, 1 - k, y, z)
                ).wait_recv()

        for off in range(1, sizes[level]):
            t_copy(level, off).wait_send()
        for q in range(sizes[level]):
            acc = acc + jnp.where(mine[level] == q, value, t_buf[level, q])
        return acc

    t_start(0, tsum)
    p2_wait(2)
    l_wait(2, l_c.at[k], l_c)

    stage(2, l_c, r_k)
    tsum = t_finish(0, tsum)
    t_start(1, tsum)

    def w_block(b, carry):
        v = total(2, b)
        own[2, b] = v
        x_send[1, b] = v.astype(BF)
        return carry

    for c in range(2):
        rs_wait(2, c)
        lax.fori_loop(c * 4, c * 4 + 4, w_block, 0)
        x_start(1, c)
    x_relay(1, 0)
    x_relay(1, 1)
    tsum = t_finish(1, tsum)
    t_start(2, tsum)
    for m in range(3):
        p1_wait_send(m)
        p2_wait_send(m)
    tsum = t_finish(2, tsum)
    trace[0, 0] = jnp.sum(tsum) * (1.0 / 1048576.0)
    x_wait(1)
    x_wait_send(0)
    x_wait_send(1)

    def o_block(b, carry):
        out[b] = (flipped(1, b) - own[2, b]).astype(BF)
        return carry

    lax.fori_loop(0, 8, o_block, 0)


def per_device(block_cols, step_dir, intersection, density, kohn_sham):
    flat = lambda a: a.reshape(8, 128, 128)
    vmem = pl.BlockSpec(memory_space=pltpu.VMEM)
    smem = pl.BlockSpec(memory_space=pltpu.SMEM)
    hbm = pl.BlockSpec(memory_space=pl.ANY)
    dma = pltpu.SemaphoreType.DMA
    blk = (128, 128)
    out, trace = pl.pallas_call(
        kernel,
        out_shape=(pltpu.VMEM((8, 128, 128), BF), jax.ShapeDtypeStruct((1, 1), F32)),
        in_specs=[hbm] * 5,
        out_specs=(vmem, smem),
        scratch_shapes=[
            pltpu.SMEM((16, 64), jnp.int32), pltpu.VMEM((8,) + blk, BF), dma((2,)),
            pltpu.VMEM((129,) + blk, BF), pltpu.VMEM((129,) + blk, BF), pltpu.VMEM((129,) + blk, BF),
            pltpu.VMEM((2, 8) + blk, BF), pltpu.VMEM((2, 8) + blk, BF), pltpu.VMEM((2, 8) + blk, BF),
            pltpu.VMEM((3, 4, 8) + blk, BF), pltpu.VMEM((3, 4, 8) + blk, BF), pltpu.VMEM((3, 8) + blk, F32),
            pltpu.VMEM((2, 8) + blk, BF), pltpu.VMEM((17,) + blk, BF), pltpu.VMEM((17,) + blk, BF),
            pltpu.VMEM((3, 8, 128), F32), pltpu.VMEM((3, 8, 8, 128), F32),
            pltpu.SMEM((128,), jnp.int32), pltpu.SMEM((8,), jnp.int32),
            dma((3, 4)), dma((3, 2)), dma((3, 4)), dma((3,)), dma((3, 2, 8)), dma((3, 4, 2)), dma((3, 2, 2)),
            dma((3, 2)), dma((3, 2)), dma((1,)), dma((3, 4, 2)), dma((3, 4, 2)), dma((2, 2, 2)), dma((2, 2)), dma((2, 2)),
            pltpu.VMEM((2, 4, 8) + blk, BF), dma((2, 2)), dma((2, 4, 2)), dma((2, 4, 4)),
            dma((3, 8)), dma((3, 8)),
        ],
        compiler_params=pltpu.CompilerParams(
            collective_id=0, has_side_effects=True, vmem_limit_bytes=63_900_000
        ),
        name="hessian",
    )(block_cols.T, flat(step_dir), flat(intersection), flat(density), flat(kohn_sham))
    return out.reshape(4, 2, 128, 128), trace.reshape(())


def solution(mesh):
    spec = P("row", "col", None, None)
    return jax.shard_map(
        per_device, mesh=mesh, in_specs=(P(), spec, spec, spec, spec), out_specs=(spec, P()), check_vma=False
    )
```

```python
import jax
import jax.numpy as jnp
from jax import lax
from jax.experimental import pallas as pl
from jax.experimental.pallas import tpu as pltpu
from jax.sharding import PartitionSpec as P

MESH = pl.DeviceIdType.MESH
BF = jnp.bfloat16
F32 = jnp.float32
ZERO = 128
TZERO = 16


def kernel(
    cols_hbm, step, inter, dens, fock_hbm, out, trace,
    cols, fock, in_sem,
    r_i, r_d, r_k, l_p, l_s, l_c, parts, landed, own, x_send, x_recv0, x_recv1, t_src, t_buf, pick, tpick,
    p1_send, p1_recv_a, p1_recv_b, p1_local, p2_send, p2_recv_a, p2_recv_b,
    l_send, l_recv, l_local, rs_send, rs_recv, x_ssem, x_rsem, x_local, relay, rl_ssem, rl_rsem, rl_fsem, t_send, t_recv,
):
    cols_copy = pltpu.make_async_copy(cols_hbm, cols, in_sem.at[0])
    cols_copy.start()
    fock_copy = pltpu.make_async_copy(fock_hbm, fock, in_sem.at[1])
    fock_copy.start()
    row = lax.axis_index("row")
    col = lax.axis_index("col")
    x, k = col // 2, col % 2
    y, z = row // 4, row % 4
    h = z // 2
    zz = z % 2

    x_recv = (x_recv0, x_recv1)

    def dev(x_, k_, y_, z_):
        return (y_ * 4 + z_, x_ * 2 + k_)

    def remote(src, dst, ssem, rsem, target):
        return pltpu.make_async_remote_copy(src, dst, ssem, rsem, device_id=target, device_id_type=MESH)

    barrier = pltpu.get_barrier_semaphore()
    for d in range(1, 8):
        pl.semaphore_signal(barrier, 1, device_id=(row, (col + d) % 8), device_id_type=MESH)
    for d in range(1, 4):
        for kk in range(2):
            pl.semaphore_signal(barrier, 1, device_id=dev(x, kk, (y + d) % 4, z), device_id_type=MESH)
            pl.semaphore_signal(barrier, 1, device_id=dev(x, kk, y, (z + d) % 4), device_id_type=MESH)
    for q in range(2):
        @pl.when((h == 1) & (x != y))
        def _():
            pl.semaphore_signal(barrier, 1, device_id=dev(y, 1, y, 2 * k + q), device_id_type=MESH)

    r_i[ZERO] = jnp.zeros((128, 128), BF)
    r_d[ZERO] = jnp.zeros((128, 128), BF)
    r_k[ZERO] = jnp.zeros((128, 128), BF)
    x_recv0[TZERO] = jnp.zeros((128, 128), BF)
    x_recv1[TZERO] = jnp.zeros((128, 128), BF)
    pl.semaphore_wait(barrier, 19 + jnp.where((x == y) & (k == 1), 6, 0))

    gathers = ((inter, r_i), (dens, r_d), (fock_hbm, r_k))

    def p1_copy(m, d):
        tile, buf = gathers[m]
        slot_a = (y * 2 + zz) * 8
        slot_b = (8 + zz * 4 + y) * 8
        kind, off = d
        if kind == "a":
            return remote(tile, buf.at[pl.ds(slot_a, 8)], p1_send.at[m, off], p1_recv_a.at[m, zz], dev(x, h, y, (z + off) % 4))
        return remote(tile, buf.at[pl.ds(slot_b, 8)], p1_send.at[m, off], p1_recv_b.at[m, y], dev(x, h, (y + off) % 4, z))

    def p1_local_copy(m):
        tile, buf = gathers[m]
        slot = jnp.where(k == 0, y * 2 + zz, 8 + zz * 4 + y) * 8
        return pltpu.make_async_copy(tile, buf.at[pl.ds(slot, 8)], p1_local.at[m])

    def p1_start(m):
        for off in (1, 3, 2, 0):
            go = (k != h) if off == 0 else True

            @pl.when((k == 0) & go)
            def _():
                p1_copy(m, ("a", off)).start()

            @pl.when((k == 1) & go)
            def _():
                p1_copy(m, ("b", off)).start()

        @pl.when(k == h)
        def _():
            p1_local_copy(m).start()

    def p1_wait_send(m):
        for off in (1, 3, 2, 0):
            go = (k != h) if off == 0 else True

            @pl.when((k == 0) & go)
            def _():
                p1_copy(m, ("a", off)).wait_send()

            @pl.when((k == 1) & go)
            def _():
                p1_copy(m, ("b", off)).wait_send()

    def recv_wait(buf, start, n, sem):
        view = buf.at[pl.ds(start, n)]
        remote(view, view, sem, sem, dev(x, 1 - k, y, z)).wait_recv()

    def p1_wait(m):
        tile, buf = gathers[m]

        @pl.when(k == h)
        def _():
            p1_local_copy(m).wait()

        for q in range(2):
            mine = (k == 0) & (h == 0) & (zz == q)

            @pl.when(jnp.logical_not(mine))
            def _():
                recv_wait(buf, (y * 2 + q) * 8, 8, p1_recv_a.at[m, q])

        for yy in range(4):
            mine = (k == 1) & (y == yy)

            @pl.when((k == h) & jnp.logical_not(mine))
            def _():
                recv_wait(buf, (8 + zz * 4 + yy) * 8, 8, p1_recv_b.at[m, yy])

    def p2_a(m, src, half, off, fwd):
        buf = gathers[m][1]
        view = buf.at[pl.ds(src * 16 + half * 8, 8)]
        ssem = p2_send.at[m, 0, fwd * 4 + half * 2 + (off == 3)]
        return remote(view, view, ssem, p2_recv_a.at[m, src, half], dev(x, k, (y + off) % 4, z))

    def p2_b(m, q, half, off, fwd):
        buf = gathers[m][1]
        view = buf.at[pl.ds(64 + q * 32 + half * 16, 16)]
        ssem = p2_send.at[m, 1, fwd * 4 + half * 2 + (off == 3)]
        return remote(view, view, ssem, p2_recv_b.at[m, q, half], dev(x, k, y, (z + off) % 4))

    ways = ((0, 1), (1, 3), (1, 1), (0, 3))

    def p2_start(m):
        for half, off in ways:
            p2_a(m, y, half, off, 0).start()

            @pl.when(k == h)
            def _():
                p2_b(m, zz, half, off, 0).start()

    def p2_wait_a(m, src, half):
        recv_wait(gathers[m][1], src * 16 + half * 8, 8, p2_recv_a.at[m, src, half])

    def p2_wait_b(m, q, half):
        recv_wait(gathers[m][1], 64 + q * 32 + half * 16, 16, p2_recv_b.at[m, q, half])

    def near(off):
        return (z + 4 - off) % 4 // 2 == k

    def p2_relay(m):
        for half, off in ways[:2]:
            src = (y + 4 - off) % 4
            p2_wait_a(m, src, half)
            p2_a(m, src, half, off, 1).start()
            q = (z + 4 - off) % 2

            @pl.when(near(off))
            def _():
                p2_wait_b(m, q, half)
                p2_b(m, q, half, off, 1).start()

    def p2_wait(m):
        for half, off in ways[2:]:
            p2_wait_a(m, (y + 4 - off) % 4, half)
            q = (z + 4 - off) % 2

            @pl.when(near(off))
            def _():
                p2_wait_b(m, q, half)
        for half in range(2):
            p2_wait_a(m, (y + 2) % 4, half)

            @pl.when(near(2))
            def _():
                p2_wait_b(m, zz, half)

    def p2_wait_send(m):
        for half, off in ways:
            p2_a(m, y, half, off, 0).wait_send()

            @pl.when(k == h)
            def _():
                p2_b(m, zz, half, off, 0).wait_send()
        for half, off in ways[:2]:
            p2_a(m, (y + 4 - off) % 4, half, off, 1).wait_send()

            @pl.when(near(off))
            def _():
                p2_b(m, (z + 4 - off) % 2, half, off, 1).wait_send()

    def l_swap(n, src, buf, c):
        part = pl.ds(c * 4, 4)
        return remote(src.at[part], buf.at[k, part], l_send.at[n, c], l_recv.at[n, c], dev(x, 1 - k, y, z))

    def l_wait(n, src, buf):
        for c in range(2):
            l_swap(n, src, buf, c).wait()

    pltpu.make_async_copy(step, l_p.at[k], l_local.at[0]).start()
    p1_start(0)
    for c in range(2):
        l_swap(0, step, l_p, c).start()
    p1_start(1)

    base = row * 4

    def make_pick(n, carry):
        i, t, s = n // 8, (n // 2) % 4, n % 2
        j = cols[(2 * t + k) * 2 + s, base + i]
        jj = jnp.maximum(j, 0)
        w, q = jj & 3, (jj >> 2) & 1
        for a in range(4):
            c = a // 2
            kk = cols[4 * x + a, base + i]
            tile = t * 2 + q if c == 0 else 8 + q * 4 + t
            block = tile * 8 + w * 2
            live = (j >= 0) & (kk >= 0)
            first = cols[4 * x + 2 * c, jj]
            second = cols[4 * x + 2 * c + 1, jj]
            got = jnp.where(first == kk, block, jnp.where(second == kk, block + 1, ZERO))
            pick[n * 4 + a] = jnp.where(live, got, ZERO)
        return carry

    def make_tpick(n, carry):
        i, s = n // 2, n % 2
        j = cols[col * 2 + s, base + i]
        jj = jnp.maximum(j, 0)
        w, q = jj & 3, (jj >> 2) & 1
        block = q * 8 + w * 2
        g = (2 * y + h) * 2
        first = cols[g, jj]
        second = cols[g + 1, jj]
        got = jnp.where(first == base + i, block, jnp.where(second == base + i, block + 1, TZERO))
        tpick[n] = jnp.where(j >= 0, got, TZERO)
        return carry

    cols_copy.wait()
    fock_copy.wait()
    lax.fori_loop(0, 32, make_pick, 0)
    lax.fori_loop(0, 8, make_tpick, 0)

    p1_wait(0)
    p2_start(0)
    p2_relay(0)
    p1_wait(1)
    p2_start(1)

    def rs_copy(n, off, c):
        part = pl.ds(c * 4, 4)
        return remote(
            parts.at[n, (x + off) % 4, part], landed.at[n, off, part], rs_send.at[n, off, c], rs_recv.at[n, off, c],
            dev((x + off) % 4, k, y, z),
        )

    def stage(n, left, right):
        def rows(off, lo, hi):
            t = (x + off) % 4

            def one_row(i, carry):
                lhs = jnp.concatenate([left[a // 2, i * 2 + a % 2] for a in range(4)], axis=1)
                rhs = jnp.concatenate(
                    [
                        jnp.concatenate([right[pick[((i * 4 + t) * 2 + s) * 4 + a]] for a in range(4)], axis=1)
                        for s in range(2)
                    ],
                    axis=0,
                )
                got = lax.dot_general(lhs, rhs, (((1,), (1,)), ((), ())), preferred_element_type=F32)
                for s in range(2):
                    block = got[:, s * 128 : (s + 1) * 128]
                    if off == 0:
                        own[n, i * 2 + s] = block
                    else:
                        parts[n, t, i * 2 + s] = block.astype(BF)
                return carry

            lax.fori_loop(lo, hi, one_row, 0)

        for c in range(2):
            for off in (2, 1, 3):
                rows(off, c * 2, c * 2 + 2)
                rs_copy(n, off, c).start()
        rows(0, 0, 4)

    def rs_wait(n, c):
        for off in (1, 3, 2):
            rs_copy(n, off, c).wait()

    def total(n, b):
        acc = own[n, b]
        for off in (1, 3, 2):
            acc = acc + landed[n, off, b].astype(F32)
        return acc

    def x_copy(n, q, c):
        return remote(
            x_send.at[n, pl.ds(c * 4, 4)], x_recv[n].at[pl.ds(zz * 8 + c * 4, 4)], x_ssem.at[n, q, c],
            x_rsem.at[n, zz], dev(y, h, x, 2 * k + q),
        )

    def x_local_copy(n, c):
        return pltpu.make_async_copy(
            x_send.at[n, pl.ds(c * 4, 4)], x_recv[n].at[pl.ds(zz * 8 + c * 4, 4)], x_local.at[n, c]
        )

    def x_self(q):
        return (x == y) & (k == h) & (zz == q)

    def to_relay(n, c):
        return remote(
            x_send.at[n, pl.ds(c * 4, 4)], relay.at[n, y, pl.ds(c * 4, 4)], rl_ssem.at[n, c], rl_rsem.at[n, y, c],
            dev(x, k, x, z),
        )

    def from_relay(n, yy, c, q):
        return remote(
            relay.at[n, yy, pl.ds(c * 4, 4)], x_recv[n].at[pl.ds(zz * 8 + c * 4, 4)], rl_fsem.at[n, yy, c * 2 + q],
            x_rsem.at[n, zz], dev(yy, h, x, 2 * k + q),
        )

    by_relay = (k == 1) & (x != y)
    is_relay = (k == 1) & (x == y)

    def x_start(n, c):
        @pl.when(by_relay)
        def _():
            to_relay(n, c).start()

        for q in range(2):
            @pl.when(jnp.logical_not(x_self(q) | by_relay))
            def _():
                x_copy(n, q, c).start()

            @pl.when(x_self(q))
            def _():
                x_local_copy(n, c).start()

    def x_relay(n, c):
        @pl.when(is_relay)
        def _():
            for o in (1, 3, 2):
                yy = (y + o) % 4
                view = relay.at[n, yy, pl.ds(c * 4, 4)]
                remote(view, view, rl_ssem.at[n, c], rl_rsem.at[n, yy, c], dev(x, 1 - k, y, z)).wait_recv()
                for q in range(2):
                    from_relay(n, yy, c, q).start()

    def x_wait(n):
        for q in range(2):
            @pl.when(jnp.logical_not(x_self(q)))
            def _():
                recv_wait(x_recv[n], q * 8, 8, x_rsem.at[n, q])

            @pl.when(x_self(q))
            def _():
                for c in range(2):
                    x_local_copy(n, c).wait()

    def x_wait_send(n):
        for c in range(2):
            for q in range(2):
                @pl.when(jnp.logical_not(x_self(q) | by_relay))
                def _():
                    x_copy(n, q, c).wait_send()

            @pl.when(by_relay)
            def _():
                to_relay(n, c).wait_send()

            @pl.when(is_relay)
            def _():
                for o in (1, 3, 2):
                    for q in range(2):
                        from_relay(n, (y + o) % 4, c, q).wait_send()

    def flipped(n, b):
        return x_recv[n][tpick[b]].astype(F32).T

    pltpu.make_async_copy(step, l_p.at[k], l_local.at[0]).wait()
    l_wait(0, step, l_p)
    p2_wait(0)
    stage(0, l_p, r_i)

    def s_block(b, carry):
        l_s[k, b] = total(0, b).astype(BF)
        return carry

    for c in range(2):
        rs_wait(0, c)
        lax.fori_loop(c * 4, c * 4 + 4, s_block, 0)
        l_swap(1, l_s.at[k], l_s, c).start()
        if c == 0:
            p2_relay(1)
            p1_start(2)
    l_wait(1, l_s.at[k], l_s)
    p2_wait(1)

    stage(1, l_s, r_d)

    def x_block(b, carry):
        v = total(1, b)
        own[1, b] = v
        x_send[0, b] = v.astype(BF)
        return carry

    for c in range(2):
        rs_wait(1, c)
        lax.fori_loop(c * 4, c * 4 + 4, x_block, 0)
        x_start(0, c)
        if c == 1:
            x_relay(0, 0)
        if c == 0:
            p1_wait(2)
            p2_start(2)
    x_relay(0, 1)
    p2_relay(2)
    x_wait(0)

    def c_block(b, acc):
        c = (-(own[1, b] + flipped(0, b))).astype(BF)
        l_c[k, b] = c
        prod = c.astype(F32) * fock[b].astype(F32)
        return acc + prod.reshape(16, 8, 128).sum(axis=0)

    tsum = jnp.zeros((8, 128), F32)
    for c in range(2):
        tsum = lax.fori_loop(c * 4, c * 4 + 4, c_block, tsum)
        l_swap(2, l_c.at[k], l_c, c).start()

    def t_copy(level, off):
        if level == 0:
            target, slot = (row, (col + off) % 8), col
        elif level == 1:
            target, slot = dev(x, k, (y + off) % 4, z), y
        else:
            target, slot = dev(x, k, y, (z + off) % 4), z
        return remote(t_src.at[level], t_buf.at[level, slot], t_send.at[level, off], t_recv.at[level, slot], target)

    sizes = (8, 4, 4)
    mine = (col, y, z)

    def t_start(level, value):
        t_src[level] = value
        for off in range(1, sizes[level]):
            t_copy(level, off).start()

    def t_finish(level, value):
        acc = jnp.zeros((8, 128), F32)
        for q in range(sizes[level]):
            @pl.when(mine[level] != q)
            def _():
                remote(
                    t_src.at[level], t_buf.at[level, q], t_recv.at[level, q], t_recv.at[level, q], dev(x, 1 - k, y, z)
                ).wait_recv()

        for off in range(1, sizes[level]):
            t_copy(level, off).wait_send()
        for q in range(sizes[level]):
            acc = acc + jnp.where(mine[level] == q, value, t_buf[level, q])
        return acc

    t_start(0, tsum)
    p2_wait(2)
    l_wait(2, l_c.at[k], l_c)

    stage(2, l_c, r_k)
    tsum = t_finish(0, tsum)
    t_start(1, tsum)

    def w_block(b, carry):
        v = total(2, b)
        own[2, b] = v
        x_send[1, b] = v.astype(BF)
        return carry

    for c in range(2):
        rs_wait(2, c)
        lax.fori_loop(c * 4, c * 4 + 4, w_block, 0)
        x_start(1, c)
        if c == 0:
            tsum = t_finish(1, tsum)
            t_start(2, tsum)
        if c == 1:
            x_relay(1, 0)
    x_relay(1, 1)
    for m in range(3):
        p1_wait_send(m)
        p2_wait_send(m)
    tsum = t_finish(2, tsum)
    trace[0, 0] = jnp.sum(tsum) * (1.0 / 1048576.0)
    x_wait(1)
    x_wait_send(0)
    x_wait_send(1)

    def o_block(b, carry):
        out[b] = (flipped(1, b) - own[2, b]).astype(BF)
        return carry

    lax.fori_loop(0, 8, o_block, 0)


def per_device(block_cols, step_dir, intersection, density, kohn_sham):
    flat = lambda a: a.reshape(8, 128, 128)
    vmem = pl.BlockSpec(memory_space=pltpu.VMEM)
    smem = pl.BlockSpec(memory_space=pltpu.SMEM)
    hbm = pl.BlockSpec(memory_space=pl.ANY)
    dma = pltpu.SemaphoreType.DMA
    blk = (128, 128)
    out, trace = pl.pallas_call(
        kernel,
        out_shape=(pltpu.VMEM((8, 128, 128), BF), jax.ShapeDtypeStruct((1, 1), F32)),
        in_specs=[hbm] * 5,
        out_specs=(vmem, smem),
        scratch_shapes=[
            pltpu.SMEM((16, 64), jnp.int32), pltpu.VMEM((8,) + blk, BF), dma((2,)),
            pltpu.VMEM((129,) + blk, BF), pltpu.VMEM((129,) + blk, BF), pltpu.VMEM((129,) + blk, BF),
            pltpu.VMEM((2, 8) + blk, BF), pltpu.VMEM((2, 8) + blk, BF), pltpu.VMEM((2, 8) + blk, BF),
            pltpu.VMEM((3, 4, 8) + blk, BF), pltpu.VMEM((3, 4, 8) + blk, BF), pltpu.VMEM((3, 8) + blk, F32),
            pltpu.VMEM((2, 8) + blk, BF), pltpu.VMEM((17,) + blk, BF), pltpu.VMEM((17,) + blk, BF),
            pltpu.VMEM((3, 8, 128), F32), pltpu.VMEM((3, 8, 8, 128), F32),
            pltpu.SMEM((128,), jnp.int32), pltpu.SMEM((8,), jnp.int32),
            dma((3, 4)), dma((3, 2)), dma((3, 4)), dma((3,)), dma((3, 2, 8)), dma((3, 4, 2)), dma((3, 2, 2)),
            dma((3, 2)), dma((3, 2)), dma((1,)), dma((3, 4, 2)), dma((3, 4, 2)), dma((2, 2, 2)), dma((2, 2)), dma((2, 2)),
            pltpu.VMEM((2, 4, 8) + blk, BF), dma((2, 2)), dma((2, 4, 2)), dma((2, 4, 4)),
            dma((3, 8)), dma((3, 8)),
        ],
        compiler_params=pltpu.CompilerParams(
            collective_id=0, has_side_effects=True, vmem_limit_bytes=63_900_000
        ),
        name="hessian",
    )(block_cols.T, flat(step_dir), flat(intersection), flat(density), flat(kohn_sham))
    return out.reshape(4, 2, 128, 128), trace.reshape(())


def solution(mesh):
    spec = P("row", "col", None, None)
    return jax.shard_map(
        per_device, mesh=mesh, in_specs=(P(), spec, spec, spec, spec), out_specs=(spec, P()), check_vma=False
    )
```

```python
import jax
import jax.numpy as jnp
from jax import lax
from jax.experimental import pallas as pl
from jax.experimental.pallas import tpu as pltpu
from jax.sharding import PartitionSpec as P

MESH = pl.DeviceIdType.MESH
BF = jnp.bfloat16
F32 = jnp.float32
ZERO = 128
TZERO = 16


def kernel(
    cols_hbm, step, inter, dens, fock_hbm, out, trace,
    cols, fock, in_sem,
    r_i, r_d, r_k, l_p, l_s, l_c, parts, landed, own, x_send, x_recv0, x_recv1, t_src, t_buf, pick, tpick,
    p1_send, p1_fsend, p1_recv_a, p1_recv_b, p1_local, p2_send, p2_recv_a, p2_recv_b,
    l_send, l_recv, l_local, rs_send, rs_recv, x_ssem, x_rsem, x_local, relay, rl_ssem, rl_rsem, rl_fsem, t_send, t_recv,
):
    cols_copy = pltpu.make_async_copy(cols_hbm, cols, in_sem.at[0])
    cols_copy.start()
    fock_copy = pltpu.make_async_copy(fock_hbm, fock, in_sem.at[1])
    fock_copy.start()
    row = lax.axis_index("row")
    col = lax.axis_index("col")
    x, k = col // 2, col % 2
    y, z = row // 4, row % 4
    h = z // 2
    zz = z % 2

    x_recv = (x_recv0, x_recv1)

    def dev(x_, k_, y_, z_):
        return (y_ * 4 + z_, x_ * 2 + k_)

    def remote(src, dst, ssem, rsem, target):
        return pltpu.make_async_remote_copy(src, dst, ssem, rsem, device_id=target, device_id_type=MESH)

    barrier = pltpu.get_barrier_semaphore()
    for d in range(1, 8):
        pl.semaphore_signal(barrier, 1, device_id=(row, (col + d) % 8), device_id_type=MESH)
    for d in range(1, 4):
        for kk in range(2):
            pl.semaphore_signal(barrier, 1, device_id=dev(x, kk, (y + d) % 4, z), device_id_type=MESH)
            pl.semaphore_signal(barrier, 1, device_id=dev(x, kk, y, (z + d) % 4), device_id_type=MESH)
    for q in range(2):
        @pl.when((h == 1) & (x != y))
        def _():
            pl.semaphore_signal(barrier, 1, device_id=dev(y, 1, y, 2 * k + q), device_id_type=MESH)

    r_i[ZERO] = jnp.zeros((128, 128), BF)
    r_d[ZERO] = jnp.zeros((128, 128), BF)
    r_k[ZERO] = jnp.zeros((128, 128), BF)
    x_recv0[TZERO] = jnp.zeros((128, 128), BF)
    x_recv1[TZERO] = jnp.zeros((128, 128), BF)
    pl.semaphore_wait(barrier, 19 + jnp.where((x == y) & (k == 1), 6, 0))

    gathers = ((inter, r_i), (dens, r_d), (fock_hbm, r_k))

    def p1_copy(m, kind, off, half):
        tile, buf = gathers[m]
        ssem = p1_send.at[m, off * 2 + half]
        part = tile.at[pl.ds(half * 4, 4)]
        if kind == "a":
            slot = buf.at[pl.ds((y * 2 + zz) * 8 + half * 4, 4)]
            return remote(part, slot, ssem, p1_recv_a.at[m, zz, half], dev(x, h, y, (z + off) % 4))
        slot = buf.at[pl.ds((8 + zz * 4 + y) * 8 + half * 4, 4)]
        return remote(part, slot, ssem, p1_recv_b.at[m, y, half], dev(x, h, (y + off) % 4, z))

    def p1_local_copy(m):
        tile, buf = gathers[m]
        slot = jnp.where(k == 0, y * 2 + zz, 8 + zz * 4 + y) * 8
        return pltpu.make_async_copy(tile, buf.at[pl.ds(slot, 8)], p1_local.at[m])

    p1_own = ((0, 1), (1, 3), (1, 1), (0, 3), (0, 0), (1, 0))
    p1_fwd = ((0, 1), (1, 3))

    def p1_each(m, act):
        for half, off in p1_own:
            go = (k != h) if off == 0 else True

            @pl.when((k == 0) & go)
            def _():
                act(p1_copy(m, "a", off, half))

            @pl.when((k == 1) & go)
            def _():
                act(p1_copy(m, "b", off, half))

    def p1_start(m):
        p1_each(m, lambda c: c.start())

        @pl.when(k == h)
        def _():
            p1_local_copy(m).start()

    def near(off):
        return (z + 4 - off) % 4 // 2 == k

    def slot_a(off):
        return (y * 2 + (z + 4 - off) % 2) * 8

    def slot_b(off):
        return (8 + zz * 4 + (y + 4 - off) % 4) * 8

    def p1_fwd_a(m, half, off):
        buf = gathers[m][1]
        view = buf.at[pl.ds(slot_a(off) + half * 4, 4)]
        q = (z + 4 - off) % 2
        return remote(view, view, p1_fsend.at[m, 0, half], p1_recv_a.at[m, q, half], dev(x, k, y, (z + off) % 4))

    def p1_fwd_b(m, half, off):
        buf = gathers[m][1]
        view = buf.at[pl.ds(slot_b(off) + half * 4, 4)]
        src = (y + 4 - off) % 4
        return remote(view, view, p1_fsend.at[m, 1, half], p1_recv_b.at[m, src, half], dev(x, k, (y + off) % 4, z))

    def p1_get_a(m, off, half):
        recv_wait(gathers[m][1], slot_a(off) + half * 4, 4, p1_recv_a.at[m, (z + 4 - off) % 2, half])

    def p1_get_b(m, off, half):
        recv_wait(gathers[m][1], slot_b(off) + half * 4, 4, p1_recv_b.at[m, (y + 4 - off) % 4, half])

    def p1_relay(m):
        for half, off in p1_fwd:
            @pl.when(near(off))
            def _():
                p1_get_a(m, off, half)
                p1_fwd_a(m, half, off).start()

            @pl.when(k == h)
            def _():
                p1_get_b(m, off, half)
                p1_fwd_b(m, half, off).start()

    def p1_wait_send(m):
        p1_each(m, lambda c: c.wait_send())
        for half, off in p1_fwd:
            @pl.when(near(off))
            def _():
                p1_fwd_a(m, half, off).wait_send()

            @pl.when(k == h)
            def _():
                p1_fwd_b(m, half, off).wait_send()

    def recv_wait(buf, start, n, sem):
        view = buf.at[pl.ds(start, n)]
        remote(view, view, sem, sem, dev(x, 1 - k, y, z)).wait_recv()

    def p1_wait(m):
        @pl.when(k == h)
        def _():
            p1_local_copy(m).wait()

        for off, half in ((1, 1), (3, 0), (2, 0), (2, 1), (0, 0), (0, 1)):
            @pl.when(near(off) & ((k != 0) if off == 0 else True))
            def _():
                p1_get_a(m, off, half)

            @pl.when((k == h) & ((k != 1) if off == 0 else True))
            def _():
                p1_get_b(m, off, half)

    def p2_a(m, src, half, off, fwd):
        buf = gathers[m][1]
        view = buf.at[pl.ds(src * 16 + half * 8, 8)]
        ssem = p2_send.at[m, 0, fwd * 4 + half * 2 + (off == 3)]
        return remote(view, view, ssem, p2_recv_a.at[m, src, half], dev(x, k, (y + off) % 4, z))

    def p2_b(m, q, half, off, fwd):
        buf = gathers[m][1]
        view = buf.at[pl.ds(64 + q * 32 + half * 16, 16)]
        ssem = p2_send.at[m, 1, fwd * 4 + half * 2 + (off == 3)]
        return remote(view, view, ssem, p2_recv_b.at[m, q, half], dev(x, k, y, (z + off) % 4))

    ways = ((0, 1), (1, 3), (1, 1), (0, 3))

    def p2_start(m):
        for half, off in ways:
            p2_a(m, y, half, off, 0).start()

            @pl.when(k == h)
            def _():
                p2_b(m, zz, half, off, 0).start()

    def p2_wait_a(m, src, half):
        recv_wait(gathers[m][1], src * 16 + half * 8, 8, p2_recv_a.at[m, src, half])

    def p2_wait_b(m, q, half):
        recv_wait(gathers[m][1], 64 + q * 32 + half * 16, 16, p2_recv_b.at[m, q, half])

    def p2_relay(m):
        for half, off in ways[:2]:
            src = (y + 4 - off) % 4
            p2_wait_a(m, src, half)
            p2_a(m, src, half, off, 1).start()
            q = (z + 4 - off) % 2

            @pl.when(near(off))
            def _():
                p2_wait_b(m, q, half)
                p2_b(m, q, half, off, 1).start()

    def p2_wait(m):
        for half, off in ways[2:]:
            p2_wait_a(m, (y + 4 - off) % 4, half)
            q = (z + 4 - off) % 2

            @pl.when(near(off))
            def _():
                p2_wait_b(m, q, half)
        for half in range(2):
            p2_wait_a(m, (y + 2) % 4, half)

            @pl.when(near(2))
            def _():
                p2_wait_b(m, zz, half)

    def p2_wait_send(m):
        for half, off in ways:
            p2_a(m, y, half, off, 0).wait_send()

            @pl.when(k == h)
            def _():
                p2_b(m, zz, half, off, 0).wait_send()
        for half, off in ways[:2]:
            p2_a(m, (y + 4 - off) % 4, half, off, 1).wait_send()

            @pl.when(near(off))
            def _():
                p2_b(m, (z + 4 - off) % 2, half, off, 1).wait_send()

    def l_swap(n, src, buf, c):
        part = pl.ds(c * 4, 4)
        return remote(src.at[part], buf.at[k, part], l_send.at[n, c], l_recv.at[n, c], dev(x, 1 - k, y, z))

    def l_wait(n, src, buf):
        for c in range(2):
            l_swap(n, src, buf, c).wait()

    pltpu.make_async_copy(step, l_p.at[k], l_local.at[0]).start()
    p1_start(0)
    for c in range(2):
        l_swap(0, step, l_p, c).start()

    p1_relay(0)
    p1_start(1)

    base = row * 4

    def make_pick(n, carry):
        i, t, s = n // 8, (n // 2) % 4, n % 2
        j = cols[(2 * t + k) * 2 + s, base + i]
        jj = jnp.maximum(j, 0)
        w, q = jj & 3, (jj >> 2) & 1
        for a in range(4):
            c = a // 2
            kk = cols[4 * x + a, base + i]
            tile = t * 2 + q if c == 0 else 8 + q * 4 + t
            block = tile * 8 + w * 2
            live = (j >= 0) & (kk >= 0)
            first = cols[4 * x + 2 * c, jj]
            second = cols[4 * x + 2 * c + 1, jj]
            got = jnp.where(first == kk, block, jnp.where(second == kk, block + 1, ZERO))
            pick[n * 4 + a] = jnp.where(live, got, ZERO)
        return carry

    def make_tpick(n, carry):
        i, s = n // 2, n % 2
        j = cols[col * 2 + s, base + i]
        jj = jnp.maximum(j, 0)
        w, q = jj & 3, (jj >> 2) & 1
        block = q * 8 + w * 2
        g = (2 * y + h) * 2
        first = cols[g, jj]
        second = cols[g + 1, jj]
        got = jnp.where(first == base + i, block, jnp.where(second == base + i, block + 1, TZERO))
        tpick[n] = jnp.where(j >= 0, got, TZERO)
        return carry

    cols_copy.wait()
    fock_copy.wait()
    lax.fori_loop(0, 32, make_pick, 0)
    lax.fori_loop(0, 8, make_tpick, 0)

    p1_wait(0)
    p2_start(0)
    p1_relay(1)
    p2_relay(0)
    p1_wait(1)
    p2_start(1)

    def rs_copy(n, off, c):
        part = pl.ds(c * 4, 4)
        return remote(
            parts.at[n, (x + off) % 4, part], landed.at[n, off, part], rs_send.at[n, off, c], rs_recv.at[n, off, c],
            dev((x + off) % 4, k, y, z),
        )

    def stage(n, left, right):
        def rows(off, lo, hi):
            t = (x + off) % 4

            def one_row(i, carry):
                lhs = jnp.concatenate([left[a // 2, i * 2 + a % 2] for a in range(4)], axis=1)
                rhs = jnp.concatenate(
                    [
                        jnp.concatenate([right[pick[((i * 4 + t) * 2 + s) * 4 + a]] for a in range(4)], axis=1)
                        for s in range(2)
                    ],
                    axis=0,
                )
                got = lax.dot_general(lhs, rhs, (((1,), (1,)), ((), ())), preferred_element_type=F32)
                for s in range(2):
                    block = got[:, s * 128 : (s + 1) * 128]
                    if off == 0:
                        own[n, i * 2 + s] = block
                    else:
                        parts[n, t, i * 2 + s] = block.astype(BF)
                return carry

            lax.fori_loop(lo, hi, one_row, 0)

        for c in range(2):
            for off in (2, 1, 3):
                rows(off, c * 2, c * 2 + 2)
                rs_copy(n, off, c).start()
        rows(0, 0, 4)

    def rs_wait(n, c):
        for off in (1, 3, 2):
            rs_copy(n, off, c).wait()

    def total(n, b):
        acc = own[n, b]
        for off in (1, 3, 2):
            acc = acc + landed[n, off, b].astype(F32)
        return acc

    def x_copy(n, q, c):
        return remote(
            x_send.at[n, pl.ds(c * 4, 4)], x_recv[n].at[pl.ds(zz * 8 + c * 4, 4)], x_ssem.at[n, q, c],
            x_rsem.at[n, zz], dev(y, h, x, 2 * k + q),
        )

    def x_local_copy(n, c):
        return pltpu.make_async_copy(
            x_send.at[n, pl.ds(c * 4, 4)], x_recv[n].at[pl.ds(zz * 8 + c * 4, 4)], x_local.at[n, c]
        )

    def x_self(q):
        return (x == y) & (k == h) & (zz == q)

    def to_relay(n, c):
        return remote(
            x_send.at[n, pl.ds(c * 4, 4)], relay.at[n, y, pl.ds(c * 4, 4)], rl_ssem.at[n, c], rl_rsem.at[n, y, c],
            dev(x, k, x, z),
        )

    def from_relay(n, yy, c, q):
        return remote(
            relay.at[n, yy, pl.ds(c * 4, 4)], x_recv[n].at[pl.ds(zz * 8 + c * 4, 4)], rl_fsem.at[n, yy, c * 2 + q],
            x_rsem.at[n, zz], dev(yy, h, x, 2 * k + q),
        )

    by_relay = (k == 1) & (x != y)
    is_relay = (k == 1) & (x == y)

    def x_start(n, c):
        @pl.when(by_relay)
        def _():
            to_relay(n, c).start()

        for q in range(2):
            @pl.when(jnp.logical_not(x_self(q) | by_relay))
            def _():
                x_copy(n, q, c).start()

            @pl.when(x_self(q))
            def _():
                x_local_copy(n, c).start()

    def x_relay(n, c):
        @pl.when(is_relay)
        def _():
            for o in (1, 3, 2):
                yy = (y + o) % 4
                view = relay.at[n, yy, pl.ds(c * 4, 4)]
                remote(view, view, rl_ssem.at[n, c], rl_rsem.at[n, yy, c], dev(x, 1 - k, y, z)).wait_recv()
                for q in range(2):
                    from_relay(n, yy, c, q).start()

    def x_wait(n):
        for q in range(2):
            @pl.when(jnp.logical_not(x_self(q)))
            def _():
                recv_wait(x_recv[n], q * 8, 8, x_rsem.at[n, q])

            @pl.when(x_self(q))
            def _():
                for c in range(2):
                    x_local_copy(n, c).wait()

    def x_wait_send(n):
        for c in range(2):
            for q in range(2):
                @pl.when(jnp.logical_not(x_self(q) | by_relay))
                def _():
                    x_copy(n, q, c).wait_send()

            @pl.when(by_relay)
            def _():
                to_relay(n, c).wait_send()

            @pl.when(is_relay)
            def _():
                for o in (1, 3, 2):
                    for q in range(2):
                        from_relay(n, (y + o) % 4, c, q).wait_send()

    def flipped(n, b):
        return x_recv[n][tpick[b]].astype(F32).T

    pltpu.make_async_copy(step, l_p.at[k], l_local.at[0]).wait()
    l_wait(0, step, l_p)
    p2_wait(0)
    stage(0, l_p, r_i)

    def s_block(b, carry):
        l_s[k, b] = total(0, b).astype(BF)
        return carry

    for c in range(2):
        rs_wait(0, c)
        lax.fori_loop(c * 4, c * 4 + 4, s_block, 0)
        l_swap(1, l_s.at[k], l_s, c).start()
        if c == 0:
            p2_relay(1)
            p1_start(2)
    p1_relay(2)
    l_wait(1, l_s.at[k], l_s)
    p2_wait(1)

    stage(1, l_s, r_d)

    def x_block(b, carry):
        v = total(1, b)
        own[1, b] = v
        x_send[0, b] = v.astype(BF)
        return carry

    for c in range(2):
        rs_wait(1, c)
        lax.fori_loop(c * 4, c * 4 + 4, x_block, 0)
        x_start(0, c)
        if c == 1:
            x_relay(0, 0)
        if c == 0:
            p1_wait(2)
            p2_start(2)
    x_relay(0, 1)
    p2_relay(2)
    x_wait(0)

    def c_block(b, acc):
        c = (-(own[1, b] + flipped(0, b))).astype(BF)
        l_c[k, b] = c
        prod = c.astype(F32) * fock[b].astype(F32)
        return acc + prod.reshape(16, 8, 128).sum(axis=0)

    tsum = jnp.zeros((8, 128), F32)
    for c in range(2):
        tsum = lax.fori_loop(c * 4, c * 4 + 4, c_block, tsum)
        l_swap(2, l_c.at[k], l_c, c).start()

    def t_copy(level, off):
        if level == 0:
            target, slot = (row, (col + off) % 8), col
        elif level == 1:
            target, slot = dev(x, k, (y + off) % 4, z), y
        else:
            target, slot = dev(x, k, y, (z + off) % 4), z
        return remote(t_src.at[level], t_buf.at[level, slot], t_send.at[level, off], t_recv.at[level, slot], target)

    sizes = (8, 4, 4)
    mine = (col, y, z)

    def t_start(level, value):
        t_src[level] = value
        for off in range(1, sizes[level]):
            t_copy(level, off).start()

    def t_finish(level, value):
        acc = jnp.zeros((8, 128), F32)
        for q in range(sizes[level]):
            @pl.when(mine[level] != q)
            def _():
                remote(
                    t_src.at[level], t_buf.at[level, q], t_recv.at[level, q], t_recv.at[level, q], dev(x, 1 - k, y, z)
                ).wait_recv()

        for off in range(1, sizes[level]):
            t_copy(level, off).wait_send()
        for q in range(sizes[level]):
            acc = acc + jnp.where(mine[level] == q, value, t_buf[level, q])
        return acc

    t_start(0, tsum)
    p2_wait(2)
    l_wait(2, l_c.at[k], l_c)

    stage(2, l_c, r_k)
    tsum = t_finish(0, tsum)
    t_start(1, tsum)

    def w_block(b, carry):
        v = total(2, b)
        own[2, b] = v
        x_send[1, b] = v.astype(BF)
        return carry

    for c in range(2):
        rs_wait(2, c)
        lax.fori_loop(c * 4, c * 4 + 4, w_block, 0)
        x_start(1, c)
        if c == 0:
            tsum = t_finish(1, tsum)
            t_start(2, tsum)
        if c == 1:
            x_relay(1, 0)
    x_relay(1, 1)
    for m in range(3):
        p1_wait_send(m)
        p2_wait_send(m)
    tsum = t_finish(2, tsum)
    trace[0, 0] = jnp.sum(tsum) * (1.0 / 1048576.0)
    x_wait(1)
    x_wait_send(0)
    x_wait_send(1)

    def o_block(b, carry):
        out[b] = (flipped(1, b) - own[2, b]).astype(BF)
        return carry

    lax.fori_loop(0, 8, o_block, 0)


def per_device(block_cols, step_dir, intersection, density, kohn_sham):
    flat = lambda a: a.reshape(8, 128, 128)
    vmem = pl.BlockSpec(memory_space=pltpu.VMEM)
    smem = pl.BlockSpec(memory_space=pltpu.SMEM)
    hbm = pl.BlockSpec(memory_space=pl.ANY)
    dma = pltpu.SemaphoreType.DMA
    blk = (128, 128)
    out, trace = pl.pallas_call(
        kernel,
        out_shape=(pltpu.VMEM((8, 128, 128), BF), jax.ShapeDtypeStruct((1, 1), F32)),
        in_specs=[hbm] * 5,
        out_specs=(vmem, smem),
        scratch_shapes=[
            pltpu.SMEM((16, 64), jnp.int32), pltpu.VMEM((8,) + blk, BF), dma((2,)),
            pltpu.VMEM((129,) + blk, BF), pltpu.VMEM((129,) + blk, BF), pltpu.VMEM((129,) + blk, BF),
            pltpu.VMEM((2, 8) + blk, BF), pltpu.VMEM((2, 8) + blk, BF), pltpu.VMEM((2, 8) + blk, BF),
            pltpu.VMEM((3, 4, 8) + blk, BF), pltpu.VMEM((3, 4, 8) + blk, BF), pltpu.VMEM((3, 8) + blk, F32),
            pltpu.VMEM((2, 8) + blk, BF), pltpu.VMEM((17,) + blk, BF), pltpu.VMEM((17,) + blk, BF),
            pltpu.VMEM((3, 8, 128), F32), pltpu.VMEM((3, 8, 8, 128), F32),
            pltpu.SMEM((128,), jnp.int32), pltpu.SMEM((8,), jnp.int32),
            dma((3, 8)), dma((3, 2, 2)), dma((3, 2, 2)), dma((3, 4, 2)), dma((3,)), dma((3, 2, 8)), dma((3, 4, 2)), dma((3, 2, 2)),
            dma((3, 2)), dma((3, 2)), dma((1,)), dma((3, 4, 2)), dma((3, 4, 2)), dma((2, 2, 2)), dma((2, 2)), dma((2, 2)),
            pltpu.VMEM((2, 4, 8) + blk, BF), dma((2, 2)), dma((2, 4, 2)), dma((2, 4, 4)),
            dma((3, 8)), dma((3, 8)),
        ],
        compiler_params=pltpu.CompilerParams(
            collective_id=0, has_side_effects=True, vmem_limit_bytes=63_900_000
        ),
        name="hessian",
    )(block_cols.T, flat(step_dir), flat(intersection), flat(density), flat(kohn_sham))
    return out.reshape(4, 2, 128, 128), trace.reshape(())


def solution(mesh):
    spec = P("row", "col", None, None)
    return jax.shard_map(
        per_device, mesh=mesh, in_specs=(P(), spec, spec, spec, spec), out_specs=(spec, P()), check_vma=False
    )
```
